128 devices in a mesh: gz: 4 (over y_hi, core), tile: 32 (over y_lo, z, x).
Axes of the slice: x: 4, y: 4 (y_hi: 2, y_lo: 2; y = y_hi * 2 + y_lo), z: 4, core: 2. Of those that a mesh axis runs over, the one named last changes fastest.
Arguments:
- density: bfloat16 [32, 256, 512], P('gz', 'tile'), may hold values from -6 to 6
- w_first: bfloat16 [8, 1, 3, 3, 3], replicated, may hold values from -1.75 to 1.75
- b_first: float32 [8], replicated, may hold values from -1.25 to 1.25
- w_second: bfloat16 [8, 8, 3, 3, 3], replicated, may hold values from -0.5 to 0.5
- b_second: float32 [8], replicated, may hold values from -1.25 to 1.25
- w_third: bfloat16 [16, 8, 3, 3, 3], replicated, may hold values from -0.5 to 0.5
- b_third: float32 [16], replicated, may hold values from -1.25 to 1.25
- w_fourth: bfloat16 [16, 16, 3, 3, 3], replicated, may hold values from -0.4375 to 0.4375
- b_fourth: float32 [16], replicated, may hold values from -1.25 to 1.25
- w_fifth: bfloat16 [8, 24, 3, 3, 3], replicated, may hold values from -0.3125 to 0.3125
- b_fifth: float32 [8], replicated, may hold values from -1.25 to 1.25
- w_sixth: bfloat16 [8, 8, 3, 3, 3], replicated, may hold values from -0.5 to 0.5
- b_sixth: float32 [8], replicated, may hold values from -1.25 to 1.25
- w_head: bfloat16 [8], replicated, may hold values from -3 to 3
- b_head: float32 [1], replicated, may hold values from -1.75 to 1.75
Outputs:
- field: float32 [32, 256, 512], P('gz', 'tile')
The draws below stay inside these ranges and needn't reach their ends.
All inputs are finite; a program needn't handle non-finite values.
Results may differ from the reference program's by a relative error of at most 0.012.
Values may be sent and summed in bfloat16 or wider, within the bound.
A program may use at most 128 MiB of HBM per device.

```python
import jax
import jax.numpy as jnp
from jax import lax

CF = 8
CC = 16
NY = 512
CJ = 24
NZ = 32
NX = 256


def block_levels(rng, shape, shards, low, top_value):
    level, own = 1.0, jax.random.fold_in(rng, 6)
    for dim, blocks in shards:
        heights = jnp.exp(jax.random.uniform(jax.random.fold_in(own, dim), (blocks,), jnp.float32, low / len(shards), top_value / len(shards)))
        level = level * jnp.repeat(heights, shape[dim] // blocks).reshape([-1 if axis == dim else 1 for axis in range(len(shape))])
    return level


def noise(own_key, extent, spread, limit, split=(), dtype=jnp.bfloat16):
    drawn = jax.random.normal(own_key, extent, jnp.float32) * spread
    if len(split) > 0:
        drawn = block_levels(own_key, extent, split, -0.22, 0.18) * drawn
    return jnp.clip(drawn, min=-limit, max=limit).astype(dtype)


def setup_inputs(seed: int = 0) -> dict:
    key_of = jax.random.split(jax.random.key(seed), 16)
    return {
        "density": noise(key_of[0], (NZ, NX, NY), 1.0, 6.0, ((0, 4), (1, 32))),
        "w_first": noise(key_of[1], (CF, 1, 3, 3, 3), 0.27, 1.75),
        "b_first": noise(key_of[2], (CF,), 0.2, 1.25, (), jnp.float32),
        "w_second": noise(key_of[3], (CF, CF, 3, 3, 3), 0.096, 0.5),
        "b_second": noise(key_of[4], (CF,), 0.2, 1.25, (), jnp.float32),
        "w_third": noise(key_of[5], (CC, CF, 3, 3, 3), 0.096, 0.5),
        "b_third": noise(key_of[6], (CC,), 0.2, 1.25, (), jnp.float32),
        "w_fourth": noise(key_of[7], (CC, CC, 3, 3, 3), 0.068, 0.4375),
        "b_fourth": noise(key_of[8], (CC,), 0.2, 1.25, (), jnp.float32),
        "w_fifth": noise(key_of[9], (CF, CJ, 3, 3, 3), 0.056, 0.3125),
        "b_fifth": noise(key_of[10], (CF,), 0.2, 1.25, (), jnp.float32),
        "w_sixth": noise(key_of[11], (CF, CF, 3, 3, 3), 0.096, 0.5),
        "b_sixth": noise(key_of[12], (CF,), 0.2, 1.25, (), jnp.float32),
        "w_head": noise(key_of[13], (CF,), 0.5, 3.0),
        "b_head": noise(key_of[14], (1,), 0.3, 1.75, (), jnp.float32),
    }


def convolve(values, weight, bias):
    padded = jnp.pad(values, ((0, 0), (1, 1), (1, 1), (1, 1)), mode="wrap")
    out = lax.conv_general_dilated(padded[None].astype(jnp.float32), weight.astype(jnp.float32), (1, 1, 1), "VALID", dimension_numbers=("NCDHW", "OIDHW", "NCDHW"), precision=lax.Precision.HIGHEST)[0]
    out = out + bias[:, None, None, None]
    return jnp.maximum(out, 0.1 * out).astype(jnp.bfloat16)


def reference(density, w_first, b_first, w_second, b_second, w_third, b_third, w_fourth, b_fourth, w_fifth, b_fifth, w_sixth, b_sixth, w_head, b_head):
    first = convolve(density[None], w_first, b_first)
    skip = convolve(first, w_second, b_second)
    chans, zlen, xlen, ylen = skip.shape
    pooled = skip.astype(jnp.float32).reshape(chans, zlen // 2, 2, xlen // 2, 2, ylen // 2, 2).mean(axis=(2, 4, 6)).astype(jnp.bfloat16)
    coarse_one = convolve(pooled, w_third, b_third)
    coarse_two = convolve(coarse_one, w_fourth, b_fourth)
    upsampled = jnp.repeat(jnp.repeat(jnp.repeat(coarse_two, 2, axis=1), 2, axis=2), 2, axis=3)
    joined = jnp.concatenate([skip, upsampled], axis=0)
    decoded = convolve(joined, w_fifth, b_fifth)
    refined = convolve(decoded, w_sixth, b_sixth)
    return jnp.einsum("c,czxy->zxy", w_head.astype(jnp.float32), refined.astype(jnp.float32), precision=lax.Precision.HIGHEST) + b_head[0]
```

```python
import jax
import jax.numpy as jnp
from jax import lax
from jax.experimental import pallas as pl
from jax.experimental.pallas import tpu as pltpu
from jax.sharding import PartitionSpec as P

MESH = pl.DeviceIdType.MESH
F32 = jnp.float32
BF16 = jnp.bfloat16

ZL = 8
XL = 8
NY = 512
NC = NY // 2
WAYS = [(-1, -1), (-1, 1), (1, -1), (1, 1), (-1, 0), (1, 0), (0, -1), (0, 1)]


def lanes(shape):
    return lax.broadcasted_iota(jnp.int32, shape, len(shape) - 1)


def column(row, count):
    eye = lax.broadcasted_iota(jnp.int32, (count, count), 0) == lanes((count, count))
    return jnp.sum(jnp.where(eye, jnp.broadcast_to(row, (count, count)), 0.0), axis=1, keepdims=True)


def act(total):
    return jnp.maximum(total, 0.1 * total)


def spread_taps(weight, width, groups):
    taps, cout, cin = weight.shape
    rows = lax.broadcasted_iota(jnp.int32, (cin, width), 0)
    table = (lanes((cin, width)) % groups == rows).astype(F32).astype(BF16)
    flat = weight.astype(F32).reshape(taps * cout, cin).astype(BF16)
    return jnp.dot(flat, table, preferred_element_type=F32).reshape(taps, cout, width)


def store_band(dst, tiles, cin, outs, ins):
    cout, width = tiles.shape[1], tiles.shape[2]
    shape = (outs, cout, width)
    place = lanes(shape) // cin - lax.broadcasted_iota(jnp.int32, shape, 0)
    for dy in range(3):
        acc = jnp.zeros(shape, F32)
        for dz in range(3):
            for dx in range(3):
                tile = jnp.broadcast_to(tiles[dz * 9 + dx * 3 + dy][None], shape)
                acc = jnp.where(place == dz * ins + dx, tile, acc)
        rows = outs * cout
        dst[dy * rows : (dy + 1) * rows, :] = acc.reshape(rows, width).astype(BF16)


def fold(partial, rows, bias):
    width = partial.shape[1]
    low = pltpu.roll(partial[:rows], 1, 1)
    high = pltpu.roll(partial[2 * rows :], width - 1, 1)
    total = partial[rows : 2 * rows] + low + high
    cout = bias.shape[0]
    total = total.reshape(rows // cout, cout, width) + bias[None]
    return act(total).reshape(rows, width).astype(BF16)


def kernel(
    d_hbm, w1_h, b1_h, w2_h, b2_h, w3_h, b3_h, w4_h, b4_h, w5_h, b5_h, w6_h, b6_h, wh_h, bh_h,
    out_ref,
    w1, b1, w2, b2, w3, b3, w4, b4, w5, b5, w6, b6, wh, bh,
    dc, dl, dr, slo, shi, rolled, first, skip, pool_ex, pooled, one, upper, deco,
    m1, m2, m2s, m3, m4, m5, m6, mh, pick, spread, bias,
    in_sem, send1, recv1, send2, recv2,
):
    gz, tile = lax.axis_size("gz"), lax.axis_size("tile")
    g, t = lax.axis_index("gz"), lax.axis_index("tile")

    def neighbour(way):
        return (lax.rem(g + way[0] + gz, gz), lax.rem(t + way[1] + tile, tile))

    load_d = pltpu.make_async_copy(d_hbm, dc.at[4:12], in_sem.at[0])
    load_d.start()
    loads = []
    pairs = zip(
        (w1_h, b1_h, w2_h, b2_h, w3_h, b3_h, w4_h, b4_h, w5_h, b5_h, w6_h, b6_h, wh_h, bh_h),
        (w1, b1, w2, b2, w3, b3, w4, b4, w5, b5, w6, b6, wh, bh),
    )
    for i, (src, dst) in enumerate(pairs):
        loads.append(pltpu.make_async_copy(src, dst, in_sem.at[1 + i]))
        loads[-1].start()

    barrier = pltpu.get_barrier_semaphore()
    for way in WAYS:
        pl.semaphore_signal(barrier, inc=1, device_id=neighbour(way), device_id_type=MESH)

    load_d.wait()
    own = dc[4:12].astype(F32)
    slo[...] = own[:, :4].astype(BF16)
    shi[...] = own[:, 4:].astype(BF16)
    pl.semaphore_wait(barrier, len(WAYS))

    edge_src = {-1: (0, 4), 0: (0, 8), 1: (4, 4)}
    edge_dst = {-1: (12, 4), 0: (4, 8), 1: (0, 4)}
    copies = []
    for k, (sz, sx) in enumerate(WAYS):
        z0, n = edge_src[sz]
        d0, _ = edge_dst[sz]
        if sx == 0:
            src, dst = dc.at[4 + z0 : 4 + z0 + n], dc.at[d0 : d0 + n]
        else:
            src = (slo if sx < 0 else shi).at[z0 : z0 + n]
            dst = (dr if sx < 0 else dl).at[d0 : d0 + n]
        copies.append(
            pltpu.make_async_remote_copy(
                src_ref=src, dst_ref=dst, send_sem=send1.at[k], recv_sem=recv1.at[k],
                device_id=neighbour((sz, sx)), device_id_type=MESH,
            )
        )
        copies[-1].start()

    for load in loads:
        load.wait()
    for k, (ref, count) in enumerate(((b1, 8), (b2, 8), (b3, 16), (b4, 16), (b5, 8), (b6, 8))):
        bias[k, :count, :] = jnp.broadcast_to(column(ref[...], count), (count, NY))

    taps = w1[...].astype(F32)
    shape = (14, 8, 256)
    lane = lanes(shape)
    slot = lane % 16
    xx = jnp.where(slot < 8, slot + 4, jnp.where(slot < 12, slot - 8, slot))
    place = lane - slot + xx - lax.broadcasted_iota(jnp.int32, shape, 0)
    acc = jnp.zeros(shape, F32)
    for dz in range(3):
        for dx in range(3):
            for dy in range(3):
                col = column(taps[dz * 3 + dx, dy : dy + 1, :], 8)
                acc = jnp.where(place == dy * 48 + dz * 16 + dx, jnp.broadcast_to(col[None], shape), acc)
    m1[...] = acc.reshape(112, 256).astype(BF16)

    tiles = spread_taps(w2[...], 256, 8)
    store_band(m2, tiles, 8, 8, 10)
    store_band(m2s, tiles, 8, 2, 4)

    rows = lax.broadcasted_iota(jnp.int32, (8, 256), 0)
    table = (lanes((8, 256)) % 8 == rows).astype(F32).astype(BF16)
    w3v = w3[...]
    tiles = jnp.stack(
        [
            lax.dot_general(w3v[k], table, (((0,), (0,)), ((), ())), preferred_element_type=F32)
            for k in range(27)
        ]
    )
    store_band(m3, tiles, 8, 8, 10)
    store_band(m4, spread_taps(w4[...], 256, 16), 16, 3, 5)

    rows = lax.broadcasted_iota(jnp.int32, (24, 256), 0)
    lane = lanes((24, 256))
    table = jnp.where(lane < 144, lane % 8, (lane - 144) % 16 + 8) == rows
    flat = w5[...].astype(F32).reshape(27 * 8, 24).astype(BF16)
    tiles = jnp.dot(flat, table.astype(F32).astype(BF16), preferred_element_type=F32)
    tiles = tiles.reshape(27, 8, 256)
    shape = (4, 8, 256)
    lane = lanes(shape)
    out_x = lax.broadcasted_iota(jnp.int32, shape, 0)
    place = jnp.where(lane < 144, lane // 8 - out_x, -1)
    coarse = jnp.where(lane >= 144, (lane - 144) // 16, -1)
    for odd in range(2):
        for dy in range(3):
            acc = jnp.zeros(shape, F32)
            for dz in range(3):
                for dx in range(3):
                    tile_v = jnp.broadcast_to(tiles[dz * 9 + dx * 3 + dy][None], shape)
                    acc = jnp.where(place == dz * 6 + dx, tile_v, acc)
                    at = ((dz + odd) // 2) * 3 + (out_x + dx) // 2
                    acc = acc + jnp.where(coarse == at, tile_v, 0.0)
            m5[odd, dy * 32 : (dy + 1) * 32, :] = acc.reshape(32, 256).astype(BF16)

    store_band(m6, spread_taps(w6[...], 256, 8), 8, 8, 10)

    rows = lax.broadcasted_iota(jnp.int32, (8, 128), 0)
    lane = lanes((8, 128))
    table = (lane % 8 == rows).astype(F32).astype(BF16)
    head = jnp.dot(wh[...], table, preferred_element_type=F32)
    mh[...] = jnp.where(lane // 8 == rows, jnp.broadcast_to(head, (8, 128)), 0.0).astype(BF16)

    rows = lax.broadcasted_iota(jnp.int32, (NY, NC), 0)
    pick[...] = jnp.where(rows // 2 == lanes((NY, NC)), 0.125, 0.0).astype(BF16)
    rows = lax.broadcasted_iota(jnp.int32, (NC, NY), 0)
    spread[...] = jnp.where(lanes((NC, NY)) // 2 == rows, 1.0, 0.0).astype(BF16)

    for copy in copies:
        copy.wait()

    @pl.loop(0, 16)
    def _(z):
        full = jnp.concatenate(
            [dc[z].astype(F32), dl[z].astype(F32), dr[z].astype(F32)], axis=0
        )
        rolled[0, z] = pltpu.roll(full, 1, 1).astype(BF16)
        rolled[1, z] = full.astype(BF16)
        rolled[2, z] = pltpu.roll(full, NY - 1, 1).astype(BF16)

    def do_first(z):
        total = jnp.dot(
            m1[:, :144], rolled[:, pl.ds(z, 3)].reshape(144, NY), preferred_element_type=F32
        )
        total = total.reshape(14, 8, NY) + bias[0, :8, :][None]
        first[z] = act(total).reshape(112, NY).astype(BF16)

    def second_own(z):
        window = first[pl.ds(z, 3), 16:96].reshape(240, NY)
        out = fold(jnp.dot(m2[:, :240], window, preferred_element_type=F32), 64, bias[1, :8, :])
        skip[z, 16:80] = out
        return out

    def second_sides(z):
        for start, to in ((0, 0), (80, 80)):
            window = first[pl.ds(z, 3), start : start + 32].reshape(96, NY)
            skip[z, to : to + 16] = fold(
                jnp.dot(m2s[:, :96], window, preferred_element_type=F32), 16, bias[1, :8, :]
            )

    @pl.loop(2, 12)
    def _(z):
        do_first(z)

    @pl.loop(0, 4)
    def _(k):
        total = None
        for half in range(2):
            out = second_own(2 + 2 * k + half)
            part = jnp.dot(out, pick[...], preferred_element_type=F32)
            total = part if total is None else total + part
        pairs_x = total.reshape(4, 2, 8, NC)
        pool_ex[3 + k, 3:7] = (pairs_x[:, 0] + pairs_x[:, 1]).astype(BF16)

    edge_src = {-1: (3, 3), 0: (3, 4), 1: (4, 3)}
    edge_dst = {-1: 7, 0: 3, 1: 0}
    copies = []
    for k, (sz, sx) in enumerate(WAYS):
        z0, nz = edge_src[sz]
        x0, nx = edge_src[sx]
        zd, xd = edge_dst[sz], edge_dst[sx]
        copies.append(
            pltpu.make_async_remote_copy(
                src_ref=pool_ex.at[z0 : z0 + nz, x0 : x0 + nx],
                dst_ref=pool_ex.at[zd : zd + nz, xd : xd + nx],
                send_sem=send2.at[k], recv_sem=recv2.at[k],
                device_id=neighbour((sz, sx)), device_id_type=MESH,
            )
        )
        copies[-1].start()

    for z in (0, 1, 12, 13):
        do_first(z)

    @pl.loop(2, 10)
    def _(z):
        second_sides(z)

    for z in (0, 1, 10, 11):
        second_own(z)
        second_sides(z)

    for copy in copies:
        copy.wait()

    @pl.loop(0, 10)
    def _(z):
        pooled[z] = pool_ex[z].astype(F32).reshape(80, NC).astype(BF16)

    @pl.loop(0, 8)
    def _(z):
        window = pooled[pl.ds(z, 3)].reshape(240, NC)
        one[z] = fold(
            jnp.dot(m3[:, :240], window, preferred_element_type=F32), 128, bias[2, :, :NC]
        )

    @pl.loop(0, 6)
    def _(z):
        for b in range(2):
            window = one[pl.ds(z, 3), 48 * b : 48 * b + 80].reshape(240, NC)
            two = fold(
                jnp.dot(m4[:, :240], window, preferred_element_type=F32), 48, bias[3, :, :NC]
            )
            upper[z, 48 * b : 48 * b + 48] = jnp.dot(
                two, spread[...], preferred_element_type=F32
            ).astype(BF16)

    @pl.loop(0, 5)
    def _(k):
        for odd in range(2):
            z = 2 * k + odd
            for start, to, lo in ((0, 0, 0), (32, 32, 0), (48, 64, 16)):
                window = jnp.concatenate(
                    [
                        skip[pl.ds(z, 3), start : start + 48].reshape(144, NY),
                        upper[pl.ds(k, 2), start : start + 48].reshape(96, NY),
                    ],
                    axis=0,
                )
                band = m5[odd, :, :240]
                if lo:
                    band = jnp.concatenate([band[16:32], band[48:64], band[80:96]], axis=0)
                n = 32 - lo
                deco[z, to : to + n] = fold(
                    jnp.dot(band, window, preferred_element_type=F32), n, bias[4, :8, :]
                )

    @pl.loop(0, 8)
    def _(z):
        window = deco[pl.ds(z, 3)].reshape(240, NY)
        refined = fold(
            jnp.dot(m6[:, :240], window, preferred_element_type=F32), 64, bias[5, :8, :]
        )
        head = jnp.dot(mh[:, :64], refined, preferred_element_type=F32)
        out_ref[z] = head + jnp.broadcast_to(bh[...], (8, NY))


def body(d, w1, b1, w2, b2, w3, b3, w4, b4, w5, b5, w6, b6, wh, bh):
    def taps(weight, order):
        turned = weight.transpose(order)
        return turned.reshape(27, turned.shape[3], turned.shape[4])

    plain, swapped = (2, 3, 4, 0, 1), (2, 3, 4, 1, 0)
    args = (
        d,
        w1.transpose(1, 2, 3, 4, 0).reshape(9, 3, 8), b1.reshape(1, 8),
        taps(w2, plain), b2.reshape(1, 8),
        taps(w3, swapped), b3.reshape(1, 16),
        taps(w4, plain), b4.reshape(1, 16),
        taps(w5, plain), b5.reshape(1, 8),
        taps(w6, plain), b6.reshape(1, 8),
        wh.reshape(1, 8), bh.reshape(1, 1),
    )
    V = pltpu.VMEM
    small = [V(a.shape, a.dtype) for a in args[1:]]
    return pl.pallas_call(
        kernel,
        out_shape=jax.ShapeDtypeStruct((ZL, XL, NY), F32),
        in_specs=[pl.BlockSpec(memory_space=pl.ANY)] * len(args),
        out_specs=pl.BlockSpec(memory_space=pltpu.VMEM),
        scratch_shapes=small
        + [
            V((16, 8, NY), BF16), V((16, 4, NY), BF16), V((16, 4, NY), BF16),
            V((8, 4, NY), BF16), V((8, 4, NY), BF16),
            V((3, 16, 16, NY), BF16),
            V((14, 112, NY), BF16), V((12, 96, NY), BF16),
            V((10, 10, 8, NC), BF16), V((10, 80, NC), BF16),
            V((8, 128, NC), BF16), V((6, 96, NY), BF16), V((10, 80, NY), BF16),
            V((112, 256), BF16), V((192, 256), BF16), V((48, 256), BF16),
            V((384, 256), BF16), V((144, 256), BF16), V((2, 96, 256), BF16),
            V((192, 256), BF16), V((8, 128), BF16),
            V((NY, NC), BF16), V((NC, NY), BF16), V((6, 16, NY), F32),
            pltpu.SemaphoreType.DMA((15,)),
            pltpu.SemaphoreType.DMA((8,)), pltpu.SemaphoreType.DMA((8,)),
            pltpu.SemaphoreType.DMA((8,)), pltpu.SemaphoreType.DMA((8,)),
        ],
        compiler_params=pltpu.CompilerParams(
            collective_id=0, has_side_effects=True, vmem_limit_bytes=48 * 1024 * 1024
        ),
        name="unet_window",
    )(*args)


def solution(mesh):
    return jax.shard_map(
        body,
        mesh=mesh,
        in_specs=(P("gz", "tile", None),) + (P(),) * 14,
        out_specs=P("gz", "tile", None),
        check_vma=False,
    )
```

```python
import jax
import jax.numpy as jnp
from jax import lax
from jax.experimental import pallas as pl
from jax.experimental.pallas import tpu as pltpu
from jax.sharding import PartitionSpec as P

MESH = pl.DeviceIdType.MESH
F32 = jnp.float32
BF16 = jnp.bfloat16

ZL = 8
XL = 8
NY = 512
NC = NY // 2
WAYS = [(-1, -1), (-1, 1), (1, -1), (1, 1), (-1, 0), (1, 0), (0, -1), (0, 1)]

U1 = 10
U2 = 4
U3 = 8
UR = 5
U4 = 8
U5 = 6
U6 = 5
U7 = 8


def lanes(shape):
    return lax.broadcasted_iota(jnp.int32, shape, len(shape) - 1)


def column(row, count):
    eye = lax.broadcasted_iota(jnp.int32, (count, count), 0) == lanes((count, count))
    return jnp.sum(jnp.where(eye, jnp.broadcast_to(row, (count, count)), 0.0), axis=1, keepdims=True)


def act(total):
    return jnp.maximum(total, 0.1 * total)


def spread_taps(weight, width, groups):
    taps, cout, cin = weight.shape
    rows = lax.broadcasted_iota(jnp.int32, (cin, width), 0)
    table = (lanes((cin, width)) % groups == rows).astype(F32).astype(BF16)
    flat = weight.astype(F32).reshape(taps * cout, cin).astype(BF16)
    return jnp.dot(flat, table, preferred_element_type=F32).reshape(taps, cout, width)


def store_band(dst, tiles, cin, outs, ins):
    cout, width = tiles.shape[1], tiles.shape[2]
    shape = (outs, cout, width)
    place = lanes(shape) // cin - lax.broadcasted_iota(jnp.int32, shape, 0)
    for dy in range(3):
        acc = jnp.zeros(shape, F32)
        for dz in range(3):
            for dx in range(3):
                tile = jnp.broadcast_to(tiles[dz * 9 + dx * 3 + dy][None], shape)
                acc = jnp.where(place == dz * ins + dx, tile, acc)
        rows = outs * cout
        dst[dy * rows : (dy + 1) * rows, :] = acc.reshape(rows, width).astype(BF16)


def loop(lo, hi, step, step_body):
    assert (hi - lo) % step == 0

    @pl.loop(0, (hi - lo) // step)
    def _(k):
        for u in range(step):
            step_body(lo + k * step + u)


def before(part):
    return jnp.concatenate([pltpu.roll(part[:, -128:], 1, 1), part[:, :-128]], axis=1)


def after(part):
    return jnp.concatenate([part[:, 128:], pltpu.roll(part[:, :128], 127, 1)], axis=1)


def fold(partial, rows, bias):
    width = partial.shape[1]
    total = partial[rows : 2 * rows] + before(partial[:rows]) + after(partial[2 * rows :])
    cout = bias.shape[0]
    bias = jnp.concatenate([bias] * (width // 128), axis=1)
    total = total.reshape(rows // cout, cout, width) + bias[None]
    return act(total).reshape(rows, width).astype(BF16)


def kernel(
    d_hbm, w1_h, b1_h, w2_h, b2_h, w3_h, b3_h, w4_h, b4_h, w5_h, b5_h, w6_h, b6_h, wh_h, bh_h,
    out_ref,
    w1, b1, w2, b2, w3, b3, w4, b4, w5, b5, w6, b6, wh, bh,
    d_in, dc, dl, dr, slo, shi, rolled, first, skip, pool_ex, pooled, one, two, deco, refined,
    m1, m2, m2s, m3, m4, m5, m6, mh, mix, unmix, bias,
    in_sem, send1, recv1, send2, recv2,
):
    gz, tile = lax.axis_size("gz"), lax.axis_size("tile")
    g, t = lax.axis_index("gz"), lax.axis_index("tile")

    def neighbour(way):
        return (lax.rem(g + way[0] + gz, gz), lax.rem(t + way[1] + tile, tile))

    barrier = pltpu.get_barrier_semaphore()
    for way in WAYS:
        pl.semaphore_signal(barrier, inc=1, device_id=neighbour(way), device_id_type=MESH)

    load_d = pltpu.make_async_copy(d_hbm, d_in, in_sem.at[0])
    load_d.start()
    loads = []
    pairs = zip(
        (w1_h, b1_h, w2_h, b2_h, w3_h, b3_h, w4_h, b4_h, w5_h, b5_h, w6_h, b6_h, wh_h, bh_h),
        (w1, b1, w2, b2, w3, b3, w4, b4, w5, b5, w6, b6, wh, bh),
    )
    for i, (src, dst) in enumerate(pairs):
        loads.append(pltpu.make_async_copy(src, dst, in_sem.at[1 + i]))
        loads[-1].start()

    rows = lax.broadcasted_iota(jnp.int32, (NY, NY), 0)
    mix[...] = jnp.where(rows % 4 * 128 + rows // 4 == lanes((NY, NY)), 1.0, 0.0).astype(BF16)
    load_d.wait()
    own = d_in[...].astype(F32).reshape(64, NY).astype(BF16)
    own = jnp.dot(own, mix[...], preferred_element_type=F32).reshape(8, 8, NY)
    dc[4:12] = own.astype(BF16)
    slo[...] = own[:, :4].astype(BF16)
    shi[...] = own[:, 4:].astype(BF16)
    pl.semaphore_wait(barrier, len(WAYS))

    edge_src = {-1: (0, 4), 0: (0, 8), 1: (4, 4)}
    edge_dst = {-1: (12, 4), 0: (4, 8), 1: (0, 4)}
    copies = []
    for k, (sz, sx) in enumerate(WAYS):
        z0, n = edge_src[sz]
        d0, _ = edge_dst[sz]
        if sx == 0:
            src, dst = dc.at[4 + z0 : 4 + z0 + n], dc.at[d0 : d0 + n]
        else:
            src = (slo if sx < 0 else shi).at[z0 : z0 + n]
            dst = (dr if sx < 0 else dl).at[d0 : d0 + n]
        copies.append(
            pltpu.make_async_remote_copy(
                src_ref=src, dst_ref=dst, send_sem=send1.at[k], recv_sem=recv1.at[k],
                device_id=neighbour((sz, sx)), device_id_type=MESH,
            )
        )
        copies[-1].start()

    for load in loads:
        load.wait()
    for k, (ref, count) in enumerate(((b1, 8), (b2, 8), (b3, 16), (b4, 16), (b5, 8), (b6, 8))):
        bias[k, :count, :] = jnp.broadcast_to(column(ref[...], count), (count, 128))

    taps = w1[...].astype(F32)
    shape = (14, 8, 256)
    lane = lanes(shape)
    slot = lane % 16
    xx = jnp.where(slot < 8, slot + 4, jnp.where(slot < 12, slot - 8, slot))
    place = lane - slot + xx - lax.broadcasted_iota(jnp.int32, shape, 0)
    acc = jnp.zeros(shape, F32)
    for dz in range(3):
        for dx in range(3):
            for dy in range(3):
                col = column(taps[dz * 3 + dx, dy : dy + 1, :], 8)
                acc = jnp.where(place == dy * 48 + dz * 16 + dx, jnp.broadcast_to(col[None], shape), acc)
    m1[...] = acc.reshape(112, 256).astype(BF16)

    tiles = spread_taps(w2[...], 256, 8)
    store_band(m2, tiles, 8, 8, 10)
    store_band(m2s, tiles, 8, 2, 4)

    rows = lax.broadcasted_iota(jnp.int32, (8, 256), 0)
    table = (lanes((8, 256)) % 8 == rows).astype(F32).astype(BF16)
    w3v = w3[...]
    tiles = jnp.stack(
        [
            lax.dot_general(w3v[k], table, (((0,), (0,)), ((), ())), preferred_element_type=F32)
            for k in range(27)
        ]
    )
    store_band(m3, tiles, 8, 8, 10)
    store_band(m4, spread_taps(w4[...], 256, 16), 16, 3, 5)

    rows = lax.broadcasted_iota(jnp.int32, (24, 256), 0)
    lane = lanes((24, 256))
    table = jnp.where(lane < 144, lane % 8, (lane - 144) % 16 + 8) == rows
    flat = w5[...].astype(F32).reshape(27 * 8, 24).astype(BF16)
    tiles = jnp.dot(flat, table.astype(F32).astype(BF16), preferred_element_type=F32)
    tiles = tiles.reshape(27, 8, 256)
    shape = (4, 8, 256)
    lane = lanes(shape)
    out_x = lax.broadcasted_iota(jnp.int32, shape, 0)
    place = jnp.where(lane < 144, lane // 8 - out_x, -1)
    coarse = jnp.where(lane >= 144, (lane - 144) // 16, -1)
    for odd in range(2):
        for dy in range(3):
            acc = jnp.zeros(shape, F32)
            for dz in range(3):
                for dx in range(3):
                    tile_v = jnp.broadcast_to(tiles[dz * 9 + dx * 3 + dy][None], shape)
                    acc = jnp.where(place == dz * 6 + dx, tile_v, acc)
                    at = ((dz + odd) // 2) * 3 + (out_x + dx) // 2
                    acc = acc + jnp.where(coarse == at, tile_v, 0.0)
            m5[odd, dy * 32 : (dy + 1) * 32, :] = acc.reshape(32, 256).astype(BF16)

    store_band(m6, spread_taps(w6[...], 256, 8), 8, 8, 10)

    rows = lax.broadcasted_iota(jnp.int32, (8, 128), 0)
    lane = lanes((8, 128))
    table = (lane % 8 == rows).astype(F32).astype(BF16)
    head = jnp.dot(wh[...], table, preferred_element_type=F32)
    mh[...] = jnp.where(lane // 8 == rows, jnp.broadcast_to(head, (8, 128)), 0.0).astype(BF16)

    lane = lanes((NY, NY))
    rows = lax.broadcasted_iota(jnp.int32, (NY, NY), 0)
    unmix[...] = jnp.where(lane % 4 * 128 + lane // 4 == rows, 1.0, 0.0).astype(BF16)

    for copy in copies:
        copy.wait()

    @pl.loop(0, 16)
    def _(z):
        full = jnp.concatenate(
            [dc[z].astype(F32), dl[z].astype(F32), dr[z].astype(F32)], axis=0
        )
        rolled[0, z] = before(full).astype(BF16)
        rolled[1, z] = full.astype(BF16)
        rolled[2, z] = after(full).astype(BF16)

    wide_bias = jnp.concatenate([bias[0, :8, :]] * 4, axis=1)

    def do_first(z):
        total = jnp.dot(
            m1[:, :144], rolled[:, pl.ds(z, 3)].reshape(144, NY), preferred_element_type=F32
        )
        total = total.reshape(14, 8, NY) + wide_bias[None]
        first[z] = act(total).reshape(112, NY).astype(BF16)

    def second_own(z):
        window = first[pl.ds(z, 3), 16:96].reshape(240, NY)
        out = fold(jnp.dot(m2[:, :240], window, preferred_element_type=F32), 64, bias[1, :8, :])
        skip[z, 16:80] = out
        return out

    def second_sides(z):
        for start, to in ((0, 0), (80, 80)):
            window = first[pl.ds(z, 3), start : start + 32].reshape(96, NY)
            skip[z, to : to + 16] = fold(
                jnp.dot(m2s[:, :96], window, preferred_element_type=F32), 16, bias[1, :8, :]
            )

    loop(2, 12, U1, do_first)
    def own_pair(k):
        total = second_own(2 + 2 * k).astype(F32) + second_own(3 + 2 * k).astype(F32)
        total = total.reshape(4, 2, 8, NY)
        total = total[:, 0] + total[:, 1]
        low = total[:, :, :128] + total[:, :, 128:256]
        high = total[:, :, 256:384] + total[:, :, 384:]
        mean = jnp.concatenate([low, high], axis=2) * 0.125
        pool_ex[3 + k, 3:7] = mean.astype(BF16)

    loop(0, 4, U2, own_pair)

    edge_src = {-1: (3, 3), 0: (3, 4), 1: (4, 3)}
    edge_dst = {-1: 7, 0: 3, 1: 0}
    copies = []
    for k, (sz, sx) in enumerate(WAYS):
        z0, nz = edge_src[sz]
        x0, nx = edge_src[sx]
        zd, xd = edge_dst[sz], edge_dst[sx]
        copies.append(
            pltpu.make_async_remote_copy(
                src_ref=pool_ex.at[z0 : z0 + nz, x0 : x0 + nx],
                dst_ref=pool_ex.at[zd : zd + nz, xd : xd + nx],
                send_sem=send2.at[k], recv_sem=recv2.at[k],
                device_id=neighbour((sz, sx)), device_id_type=MESH,
            )
        )
        copies[-1].start()

    for z in (0, 1, 12, 13):
        do_first(z)
    loop(2, 10, U3, second_sides)
    for z in (0, 1, 10, 11):
        second_own(z)
        second_sides(z)

    for copy in copies:
        copy.wait()

    def repack(z):
        pooled[z] = pool_ex[z].astype(F32).reshape(80, NC).astype(BF16)

    def coarse_one(z):
        window = pooled[pl.ds(z, 3)].reshape(240, NC)
        one[z] = fold(
            jnp.dot(m3[:, :240], window, preferred_element_type=F32), 128, bias[2]
        )

    def coarse_two(z):
        for b in range(2):
            window = one[pl.ds(z, 3), 48 * b : 48 * b + 80].reshape(240, NC)
            two[z, 48 * b : 48 * b + 48] = fold(
                jnp.dot(m4[:, :240], window, preferred_element_type=F32), 48, bias[3]
            )

    def repeat_y(part):
        return jnp.concatenate([part[:, :128]] * 2 + [part[:, 128:]] * 2, axis=1)

    def fifth(k):
        for odd in range(2):
            z = 2 * k + odd
            for start, to, lo in ((0, 0, 0), (32, 32, 0), (48, 64, 16)):
                window = jnp.concatenate(
                    [
                        skip[pl.ds(z, 3), start : start + 48].reshape(144, NY),
                        repeat_y(two[pl.ds(k, 2), start : start + 48].reshape(96, NC)),
                    ],
                    axis=0,
                )
                band = m5[odd, :, :240]
                if lo:
                    band = jnp.concatenate([band[16:32], band[48:64], band[80:96]], axis=0)
                n = 32 - lo
                deco[z, to : to + n] = fold(
                    jnp.dot(band, window, preferred_element_type=F32), n, bias[4, :8, :]
                )

    def sixth(z):
        window = deco[pl.ds(z, 3)].reshape(240, NY)
        refined[z] = fold(
            jnp.dot(m6[:, :240], window, preferred_element_type=F32), 64, bias[5, :8, :]
        )

    loop(0, 10, UR, repack)
    loop(0, 8, U4, coarse_one)
    loop(0, 6, U5, coarse_two)
    loop(0, 5, U6, fifth)
    loop(0, 8, U7, sixth)
    head = jnp.concatenate(
        [jnp.dot(mh[:, :64], refined[z], preferred_element_type=F32) for z in range(8)], axis=0
    )
    head = head + jnp.broadcast_to(bh[...], (64, NY))
    parts = []
    for _ in range(3):
        parts.append(head.astype(BF16))
        head = head - parts[-1].astype(F32)
    plain = jnp.dot(jnp.concatenate(parts, axis=0), unmix[...], preferred_element_type=F32)
    out_ref[...] = (plain[:64] + plain[64:128] + plain[128:]).reshape(8, 8, NY)


def body(d, w1, b1, w2, b2, w3, b3, w4, b4, w5, b5, w6, b6, wh, bh):
    def taps(weight, order):
        turned = weight.transpose(order)
        return turned.reshape(27, turned.shape[3], turned.shape[4])

    plain, swapped = (2, 3, 4, 0, 1), (2, 3, 4, 1, 0)
    args = (
        d,
        w1.transpose(1, 2, 3, 4, 0).reshape(9, 3, 8), b1.reshape(1, 8),
        taps(w2, plain), b2.reshape(1, 8),
        taps(w3, swapped), b3.reshape(1, 16),
        taps(w4, plain), b4.reshape(1, 16),
        taps(w5, plain), b5.reshape(1, 8),
        taps(w6, plain), b6.reshape(1, 8),
        wh.reshape(1, 8), bh.reshape(1, 1),
    )
    V = pltpu.VMEM
    small = [V(a.shape, a.dtype) for a in args[1:]]
    return pl.pallas_call(
        kernel,
        out_shape=jax.ShapeDtypeStruct((ZL, XL, NY), F32),
        in_specs=[pl.BlockSpec(memory_space=pl.ANY)] * len(args),
        out_specs=pl.BlockSpec(memory_space=pltpu.VMEM),
        scratch_shapes=small
        + [
            V((8, 8, NY), BF16), V((16, 8, NY), BF16), V((16, 4, NY), BF16), V((16, 4, NY), BF16),
            V((8, 4, NY), BF16), V((8, 4, NY), BF16),
            V((3, 16, 16, NY), BF16),
            V((14, 112, NY), BF16), V((12, 96, NY), BF16),
            V((10, 10, 8, NC), BF16), V((10, 80, NC), BF16),
            V((8, 128, NC), BF16), V((6, 96, NC), BF16), V((10, 80, NY), BF16), V((8, 64, NY), BF16),
            V((112, 256), BF16), V((192, 256), BF16), V((48, 256), BF16),
            V((384, 256), BF16), V((144, 256), BF16), V((2, 96, 256), BF16),
            V((192, 256), BF16), V((8, 128), BF16),
            V((NY, NY), BF16), V((NY, NY), BF16), V((6, 16, 128), F32),
            pltpu.SemaphoreType.DMA((15,)),
            pltpu.SemaphoreType.DMA((8,)), pltpu.SemaphoreType.DMA((8,)),
            pltpu.SemaphoreType.DMA((8,)), pltpu.SemaphoreType.DMA((8,)),
        ],
        compiler_params=pltpu.CompilerParams(
            collective_id=0, has_side_effects=True, vmem_limit_bytes=67043328
        ),
        name="unet_window",
    )(*args)


def solution(mesh):
    return jax.shard_map(
        body,
        mesh=mesh,
        in_specs=(P("gz", "tile", None),) + (P(),) * 14,
        out_specs=P("gz", "tile", None),
        check_vma=False,
    )
```

```python
import jax
import jax.numpy as jnp
from jax import lax
from jax.experimental import pallas as pl
from jax.experimental.pallas import tpu as pltpu
from jax.sharding import PartitionSpec as P

MESH = pl.DeviceIdType.MESH
F32 = jnp.float32
BF16 = jnp.bfloat16

ZL = 8
XL = 8
NY = 512
NC = NY // 2
WAYS = [(-1, -1), (-1, 1), (1, -1), (1, 1), (-1, 0), (1, 0), (0, -1), (0, 1)]

UR = 5
U4 = 8
U5 = 6
U6 = 5
U7 = 8


def lanes(shape):
    return lax.broadcasted_iota(jnp.int32, shape, len(shape) - 1)


def column(row, count):
    eye = lax.broadcasted_iota(jnp.int32, (count, count), 0) == lanes((count, count))
    return jnp.sum(jnp.where(eye, jnp.broadcast_to(row, (count, count)), 0.0), axis=1, keepdims=True)


def act(total):
    return jnp.maximum(total, 0.1 * total)


def spread_taps(weight, width, groups):
    taps, cout, cin = weight.shape
    rows = lax.broadcasted_iota(jnp.int32, (cin, width), 0)
    table = (lanes((cin, width)) % groups == rows).astype(F32).astype(BF16)
    flat = weight.astype(F32).reshape(taps * cout, cin).astype(BF16)
    return jnp.dot(flat, table, preferred_element_type=F32).reshape(taps, cout, width)


def store_band(dst, tiles, cin, outs, ins):
    cout, width = tiles.shape[1], tiles.shape[2]
    shape = (outs, cout, width)
    place = lanes(shape) // cin - lax.broadcasted_iota(jnp.int32, shape, 0)
    for dy in range(3):
        acc = jnp.zeros(shape, F32)
        for dz in range(3):
            for dx in range(3):
                tile = jnp.broadcast_to(tiles[dz * 9 + dx * 3 + dy][None], shape)
                acc = jnp.where(place == dz * ins + dx, tile, acc)
        rows = outs * cout
        dst[dy * rows : (dy + 1) * rows, :] = acc.reshape(rows, width).astype(BF16)


def loop(lo, hi, step, step_body):
    assert (hi - lo) % step == 0

    @pl.loop(0, (hi - lo) // step)
    def _(k):
        for u in range(step):
            step_body(lo + k * step + u)


def before(part):
    return jnp.concatenate([pltpu.roll(part[:, -128:], 1, 1), part[:, :-128]], axis=1)


def after(part):
    return jnp.concatenate([part[:, 128:], pltpu.roll(part[:, :128], 127, 1)], axis=1)


def fold(partial, rows, bias):
    width = partial.shape[1]
    total = partial[rows : 2 * rows] + before(partial[:rows]) + after(partial[2 * rows :])
    cout = bias.shape[0]
    bias = jnp.concatenate([bias] * (width // 128), axis=1)
    total = total.reshape(rows // cout, cout, width) + bias[None]
    return act(total).reshape(rows, width).astype(BF16)


def kernel(
    d_hbm, w1_h, b1_h, w2_h, b2_h, w3_h, b3_h, w4_h, b4_h, w5_h, b5_h, w6_h, b6_h, wh_h, bh_h,
    out_ref,
    w1, b1, w2, b2, w3, b3, w4, b4, w5, b5, w6, b6, wh, bh,
    d_in, dc, dl, dr, slo, shi, own_y, rim_y, first, skip, pool_ex, pooled, one, two, deco, refined,
    m1, m2, m3, m4, m5, m6, mh, mix, unmix, bias,
    in_sem, send1, recv1, send2, recv2,
):
    gz, tile = lax.axis_size("gz"), lax.axis_size("tile")
    g, t = lax.axis_index("gz"), lax.axis_index("tile")

    def neighbour(way):
        return (lax.rem(g + way[0] + gz, gz), lax.rem(t + way[1] + tile, tile))

    barrier = pltpu.get_barrier_semaphore()
    for way in WAYS:
        pl.semaphore_signal(barrier, inc=1, device_id=neighbour(way), device_id_type=MESH)

    load_d = pltpu.make_async_copy(d_hbm, d_in, in_sem.at[0])
    load_d.start()
    loads = []
    pairs = zip(
        (w1_h, b1_h, w2_h, b2_h, w3_h, b3_h, w4_h, b4_h, w5_h, b5_h, w6_h, b6_h, wh_h, bh_h),
        (w1, b1, w2, b2, w3, b3, w4, b4, w5, b5, w6, b6, wh, bh),
    )
    for i, (src, dst) in enumerate(pairs):
        loads.append(pltpu.make_async_copy(src, dst, in_sem.at[1 + i]))
        loads[-1].start()

    rows = lax.broadcasted_iota(jnp.int32, (NY, NY), 0)
    mix[...] = jnp.where(rows % 4 * 128 + rows // 4 == lanes((NY, NY)), 1.0, 0.0).astype(BF16)
    load_d.wait()
    own = d_in[...].astype(F32).reshape(64, NY).astype(BF16)
    own = jnp.dot(own, mix[...], preferred_element_type=F32).reshape(8, 8, NY)
    dc[4:12] = own.astype(BF16)
    slo[...] = own[:, :4].astype(BF16)
    shi[...] = own[:, 4:].astype(BF16)
    pl.semaphore_wait(barrier, len(WAYS))

    edge_src = {-1: (0, 4), 0: (0, 8), 1: (4, 4)}
    edge_dst = {-1: (12, 4), 0: (4, 8), 1: (0, 4)}
    copies = []
    for k, (sz, sx) in enumerate(WAYS):
        z0, n = edge_src[sz]
        d0, _ = edge_dst[sz]
        if sx == 0:
            src, dst = dc.at[4 + z0 : 4 + z0 + n], dc.at[d0 : d0 + n]
        else:
            src = (slo if sx < 0 else shi).at[z0 : z0 + n]
            dst = (dr if sx < 0 else dl).at[d0 : d0 + n]
        copies.append(
            pltpu.make_async_remote_copy(
                src_ref=src, dst_ref=dst, send_sem=send1.at[k], recv_sem=recv1.at[k],
                device_id=neighbour((sz, sx)), device_id_type=MESH,
            )
        )
        copies[-1].start()

    for load in loads:
        load.wait()
    for k, (ref, count) in enumerate(((b1, 8), (b2, 8), (b3, 16), (b4, 16), (b5, 8), (b6, 8))):
        bias[k, :count, :] = jnp.broadcast_to(column(ref[...], count), (count, 128))

    taps = w1[...].astype(F32)
    shape = (14, 8, 256)
    lane = lanes(shape)
    slot = lane % 8
    rim = jnp.where(slot < 4, slot, slot + 8)
    xx = jnp.where(lane < 96, slot + 4, rim) - lax.broadcasted_iota(jnp.int32, shape, 0)
    place = jnp.where((xx >= 0) & (xx < 3), lane % 96 // 8 * 8 + xx, -1)
    acc = jnp.zeros(shape, F32)
    for dz in range(3):
        for dx in range(3):
            for dy in range(3):
                col = column(taps[dz * 3 + dx, dy : dy + 1, :], 8)
                acc = jnp.where(place == dz * 32 + dy * 8 + dx, jnp.broadcast_to(col[None], shape), acc)
    m1[...] = acc.reshape(112, 256).astype(BF16)

    tiles = spread_taps(w2[...], 256, 8)
    store_band(m2, tiles, 8, 4, 6)

    rows = lax.broadcasted_iota(jnp.int32, (8, 256), 0)
    table = (lanes((8, 256)) % 8 == rows).astype(F32).astype(BF16)
    w3v = w3[...]
    tiles = jnp.stack(
        [
            lax.dot_general(w3v[k], table, (((0,), (0,)), ((), ())), preferred_element_type=F32)
            for k in range(27)
        ]
    )
    store_band(m3, tiles, 8, 8, 10)
    store_band(m4, spread_taps(w4[...], 256, 16), 16, 3, 5)

    rows = lax.broadcasted_iota(jnp.int32, (24, 256), 0)
    lane = lanes((24, 256))
    table = jnp.where(lane < 144, lane % 8, (lane - 144) % 16 + 8) == rows
    flat = w5[...].astype(F32).reshape(27 * 8, 24).astype(BF16)
    tiles = jnp.dot(flat, table.astype(F32).astype(BF16), preferred_element_type=F32)
    tiles = tiles.reshape(27, 8, 256)
    shape = (4, 8, 256)
    lane = lanes(shape)
    out_x = lax.broadcasted_iota(jnp.int32, shape, 0)
    place = jnp.where(lane < 144, lane // 8 - out_x, -1)
    coarse = jnp.where(lane >= 144, (lane - 144) // 16, -1)
    for odd in range(2):
        for dy in range(3):
            acc = jnp.zeros(shape, F32)
            for dz in range(3):
                for dx in range(3):
                    tile_v = jnp.broadcast_to(tiles[dz * 9 + dx * 3 + dy][None], shape)
                    acc = jnp.where(place == dz * 6 + dx, tile_v, acc)
                    at = ((dz + odd) // 2) * 3 + (out_x + dx) // 2
                    acc = acc + jnp.where(coarse == at, tile_v, 0.0)
            m5[odd, dy * 32 : (dy + 1) * 32, :] = acc.reshape(32, 256).astype(BF16)

    store_band(m6, spread_taps(w6[...], 256, 8), 8, 8, 10)

    rows = lax.broadcasted_iota(jnp.int32, (8, 128), 0)
    lane = lanes((8, 128))
    table = (lane % 8 == rows).astype(F32).astype(BF16)
    head = jnp.dot(wh[...], table, preferred_element_type=F32)
    mh[...] = jnp.where(lane // 8 == rows, jnp.broadcast_to(head, (8, 128)), 0.0).astype(BF16)

    lane = lanes((NY, NY))
    rows = lax.broadcasted_iota(jnp.int32, (NY, NY), 0)
    unmix[...] = jnp.where(lane % 4 * 128 + lane // 4 == rows, 1.0, 0.0).astype(BF16)

    wide_bias = jnp.concatenate([bias[0, :8, :]] * 4, axis=1)

    def turn(dst, z, rows8):
        part = [before(rows8), rows8, after(rows8), jnp.zeros_like(rows8)]
        dst[z] = jnp.concatenate(part, axis=0).astype(BF16)

    def turn_own(z):
        turn(own_y, z, dc[z].astype(F32))

    def turn_rim(z):
        turn(rim_y, z, jnp.concatenate([dl[z].astype(F32), dr[z].astype(F32)], axis=0))

    def first_own(z):
        total = jnp.dot(
            m1[32:80, :96], own_y[pl.ds(z, 3)].reshape(96, NY), preferred_element_type=F32
        )
        first[z, 32:80] = act(total.reshape(6, 8, NY) + wide_bias[None]).reshape(48, NY).astype(BF16)

    def first_rim(z):
        band = jnp.concatenate([m1[0:32, :192], m1[80:112, :192]], axis=0)
        window = jnp.concatenate(
            [own_y[pl.ds(z, 3)].reshape(96, NY), rim_y[pl.ds(z, 3)].reshape(96, NY)], axis=0
        )
        total = jnp.dot(band, window, preferred_element_type=F32).reshape(8, 8, NY)
        out = act(total + wide_bias[None]).reshape(64, NY).astype(BF16)
        first[z, 0:32] = out[:32]
        first[z, 80:112] = out[32:]

    def second(z, b):
        window = first[pl.ds(z, 3), 32 * b : 32 * b + 48].reshape(144, NY)
        out = fold(jnp.dot(m2[:, :144], window, preferred_element_type=F32), 32, bias[1, :8, :])
        skip[z, 32 * b : 32 * b + 32] = out
        return out.astype(F32)

    def pool(k, b):
        total = (second(2 * k, b) + second(2 * k + 1, b)).reshape(2, 2, 8, NY)
        total = total[:, 0] + total[:, 1]
        low = total[:, :, :128] + total[:, :, 128:256]
        high = total[:, :, 256:384] + total[:, :, 384:]
        mean = jnp.concatenate([low, high], axis=2) * 0.125
        pool_ex[2 + k, 2 + 2 * b : 4 + 2 * b] = mean.astype(BF16)

    pool_src = {-1: (4, 6), 0: (2, 8), 1: (4, 6)}
    pool_dst = {-1: (8, 10), 0: (2, 8), 1: (0, 2)}
    copies2 = []
    for k, (sz, sx) in enumerate(WAYS):
        (z0, z1), (x0, x1) = pool_src[sz], pool_src[sx]
        (y0, y1), (u0, u1) = pool_dst[sz], pool_dst[sx]
        copies2.append(
            pltpu.make_async_remote_copy(
                src_ref=pool_ex.at[z0:z1, x0:x1],
                dst_ref=pool_ex.at[y0:y1, u0:u1],
                send_sem=send2.at[k], recv_sem=recv2.at[k],
                device_id=neighbour((sz, sx)), device_id_type=MESH,
            )
        )

    for k, (sz, sx) in enumerate(WAYS):
        if sx == 0:
            copies[k].wait_recv()
    for z in range(16):
        turn_own(z)
    for z in range(14):
        first_own(z)
    for k in range(6):
        pool(k, 1)
    for k, (sz, sx) in enumerate(WAYS):
        if sx != 0:
            copies2[k].start()

    for k, (sz, sx) in enumerate(WAYS):
        if sx != 0:
            copies[k].wait_recv()
    for z in range(4, 12):
        turn_rim(z)
    for z in range(4, 10):
        first_rim(z)
    for k in (2, 3):
        pool(k, 0)
        pool(k, 2)
    for k, (sz, sx) in enumerate(WAYS):
        if sx == 0:
            copies2[k].start()

    for z in (0, 1, 2, 3, 12, 13, 14, 15):
        turn_rim(z)
    for z in (0, 1, 2, 3, 10, 11, 12, 13):
        first_rim(z)
    for k in (0, 1, 4, 5):
        pool(k, 0)
        pool(k, 2)

    for copy in copies:
        copy.wait_send()
    for copy in copies2:
        copy.wait()

    def repack(z):
        pooled[z] = pool_ex[z].astype(F32).reshape(80, NC).astype(BF16)

    def coarse_one(z):
        window = pooled[pl.ds(z, 3)].reshape(240, NC)
        one[z] = fold(
            jnp.dot(m3[:, :240], window, preferred_element_type=F32), 128, bias[2]
        )

    def coarse_two(z):
        for b in range(2):
            window = one[pl.ds(z, 3), 48 * b : 48 * b + 80].reshape(240, NC)
            two[z, 48 * b : 48 * b + 48] = fold(
                jnp.dot(m4[:, :240], window, preferred_element_type=F32), 48, bias[3]
            )

    def repeat_y(part):
        return jnp.concatenate([part[:, :128]] * 2 + [part[:, 128:]] * 2, axis=1)

    def fifth(k):
        for odd in range(2):
            z = 2 * k + odd
            for start, to, lo in ((0, 0, 0), (32, 32, 0), (48, 64, 16)):
                window = jnp.concatenate(
                    [
                        skip[pl.ds(z, 3), start : start + 48].reshape(144, NY),
                        repeat_y(two[pl.ds(k, 2), start : start + 48].reshape(96, NC)),
                    ],
                    axis=0,
                )
                band = m5[odd, :, :240]
                if lo:
                    band = jnp.concatenate([band[16:32], band[48:64], band[80:96]], axis=0)
                n = 32 - lo
                deco[z, to : to + n] = fold(
                    jnp.dot(band, window, preferred_element_type=F32), n, bias[4, :8, :]
                )

    def sixth(z):
        window = deco[pl.ds(z, 3)].reshape(240, NY)
        refined[z] = fold(
            jnp.dot(m6[:, :240], window, preferred_element_type=F32), 64, bias[5, :8, :]
        )

    loop(0, 10, UR, repack)
    loop(0, 8, U4, coarse_one)
    loop(0, 6, U5, coarse_two)
    loop(0, 5, U6, fifth)
    loop(0, 8, U7, sixth)
    head = jnp.concatenate(
        [jnp.dot(mh[:, :64], refined[z], preferred_element_type=F32) for z in range(8)], axis=0
    )
    head = head + jnp.broadcast_to(bh[...], (64, NY))
    parts = []
    for _ in range(3):
        parts.append(head.astype(BF16))
        head = head - parts[-1].astype(F32)
    plain = jnp.dot(jnp.concatenate(parts, axis=0), unmix[...], preferred_element_type=F32)
    out_ref[...] = (plain[:64] + plain[64:128] + plain[128:]).reshape(8, 8, NY)


def body(d, w1, b1, w2, b2, w3, b3, w4, b4, w5, b5, w6, b6, wh, bh):
    def taps(weight, order):
        turned = weight.transpose(order)
        return turned.reshape(27, turned.shape[3], turned.shape[4])

    plain, swapped = (2, 3, 4, 0, 1), (2, 3, 4, 1, 0)
    args = (
        d,
        w1.transpose(1, 2, 3, 4, 0).reshape(9, 3, 8), b1.reshape(1, 8),
        taps(w2, plain), b2.reshape(1, 8),
        taps(w3, swapped), b3.reshape(1, 16),
        taps(w4, plain), b4.reshape(1, 16),
        taps(w5, plain), b5.reshape(1, 8),
        taps(w6, plain), b6.reshape(1, 8),
        wh.reshape(1, 8), bh.reshape(1, 1),
    )
    V = pltpu.VMEM
    small = [V(a.shape, a.dtype) for a in args[1:]]
    return pl.pallas_call(
        kernel,
        out_shape=jax.ShapeDtypeStruct((ZL, XL, NY), F32),
        in_specs=[pl.BlockSpec(memory_space=pl.ANY)] * len(args),
        out_specs=pl.BlockSpec(memory_space=pltpu.VMEM),
        scratch_shapes=small
        + [
            V((8, 8, NY), BF16), V((16, 8, NY), BF16), V((16, 4, NY), BF16), V((16, 4, NY), BF16),
            V((8, 4, NY), BF16), V((8, 4, NY), BF16),
            V((16, 32, NY), BF16), V((16, 32, NY), BF16),
            V((14, 112, NY), BF16), V((12, 96, NY), BF16),
            V((10, 10, 8, NC), BF16), V((10, 80, NC), BF16),
            V((8, 128, NC), BF16), V((6, 96, NC), BF16), V((10, 80, NY), BF16), V((8, 64, NY), BF16),
            V((112, 256), BF16), V((96, 256), BF16),
            V((384, 256), BF16), V((144, 256), BF16), V((2, 96, 256), BF16),
            V((192, 256), BF16), V((8, 128), BF16),
            V((NY, NY), BF16), V((NY, NY), BF16), V((6, 16, 128), F32),
            pltpu.SemaphoreType.DMA((15,)),
            pltpu.SemaphoreType.DMA((8,)), pltpu.SemaphoreType.DMA((8,)),
            pltpu.SemaphoreType.DMA((8,)), pltpu.SemaphoreType.DMA((8,)),
        ],
        compiler_params=pltpu.CompilerParams(
            collective_id=0, has_side_effects=True, vmem_limit_bytes=67043328
        ),
        name="unet_window",
    )(*args)


def solution(mesh):
    return jax.shard_map(
        body,
        mesh=mesh,
        in_specs=(P("gz", "tile", None),) + (P(),) * 14,
        out_specs=P("gz", "tile", None),
        check_vma=False,
    )
```

```python
import jax
import jax.numpy as jnp
from jax import lax
from jax.experimental import pallas as pl
from jax.experimental.pallas import tpu as pltpu
from jax.sharding import PartitionSpec as P

MESH = pl.DeviceIdType.MESH
F32 = jnp.float32
BF16 = jnp.bfloat16

ZL = 8
XL = 8
NY = 512
NC = NY // 2
WAYS = [(-1, -1), (-1, 1), (1, -1), (1, 1), (-1, 0), (1, 0), (0, -1), (0, 1)]

UR = 5
U4 = 8
U5 = 6
U6 = 5
U7 = 8


def lanes(shape):
    return lax.broadcasted_iota(jnp.int32, shape, len(shape) - 1)


def column(row, count):
    eye = lax.broadcasted_iota(jnp.int32, (count, count), 0) == lanes((count, count))
    return jnp.sum(jnp.where(eye, jnp.broadcast_to(row, (count, count)), 0.0), axis=1, keepdims=True)


def act(total):
    return jnp.maximum(total, 0.1 * total)


def spread_taps(weight, width, groups):
    taps, cout, cin = weight.shape
    rows = lax.broadcasted_iota(jnp.int32, (cin, width), 0)
    table = (lanes((cin, width)) % groups == rows).astype(F32).astype(BF16)
    flat = weight.astype(F32).reshape(taps * cout, cin).astype(BF16)
    return jnp.dot(flat, table, preferred_element_type=F32).reshape(taps, cout, width)


def store_band(dst, tiles, cin, outs, ins):
    cout, width = tiles.shape[1], tiles.shape[2]
    shape = (outs, cout, width)
    place = lanes(shape) // cin - lax.broadcasted_iota(jnp.int32, shape, 0)
    for dy in range(3):
        acc = jnp.zeros(shape, F32)
        for dz in range(3):
            for dx in range(3):
                tile = jnp.broadcast_to(tiles[dz * 9 + dx * 3 + dy][None], shape)
                acc = jnp.where(place == dz * ins + dx, tile, acc)
        rows = outs * cout
        dst[dy * rows : (dy + 1) * rows, :] = acc.reshape(rows, width).astype(BF16)


def loop(lo, hi, step, step_body):
    assert (hi - lo) % step == 0

    @pl.loop(0, (hi - lo) // step)
    def _(k):
        for u in range(step):
            step_body(lo + k * step + u)


def before(part):
    return jnp.concatenate([pltpu.roll(part[:, -128:], 1, 1), part[:, :-128]], axis=1)


def after(part):
    return jnp.concatenate([part[:, 128:], pltpu.roll(part[:, :128], 127, 1)], axis=1)


def gather(partial, rows, bias):
    width = partial.shape[1]
    total = partial[rows : 2 * rows] + before(partial[:rows]) + after(partial[2 * rows :])
    cout = bias.shape[0]
    bias = jnp.concatenate([bias] * (width // 128), axis=1)
    total = total.reshape(rows // cout, cout, width) + bias[None]
    return total.reshape(rows, width)


def fold(partial, rows, bias):
    return act(gather(partial, rows, bias)).astype(BF16)


def kernel(
    d_hbm, w1_h, b1_h, w2_h, b2_h, w3_h, b3_h, w4_h, b4_h, w5_h, b5_h, w6_h, b6_h, wh_h, bh_h,
    out_ref,
    w1, b1, w2, b2, w3, b3, w4, b4, w5, b5, w6, b6, wh, bh,
    d_in, dc, dl, dr, slo, shi, own_y, rim_y, first, skip, pool_ex, pooled, one, two, fine, deco, refined,
    m1, m2, m3, m4, m5, m5c, m6, mh, mix, unmix, bias,
    in_sem, send1, recv1, send2, recv2,
):
    gz, tile = lax.axis_size("gz"), lax.axis_size("tile")
    g, t = lax.axis_index("gz"), lax.axis_index("tile")

    def neighbour(way):
        return (lax.rem(g + way[0] + gz, gz), lax.rem(t + way[1] + tile, tile))

    barrier = pltpu.get_barrier_semaphore()
    for way in WAYS:
        pl.semaphore_signal(barrier, inc=1, device_id=neighbour(way), device_id_type=MESH)

    load_d = pltpu.make_async_copy(d_hbm, d_in, in_sem.at[0])
    load_d.start()
    loads = []
    pairs = zip(
        (w1_h, b1_h, w2_h, b2_h, w3_h, b3_h, w4_h, b4_h, w5_h, b5_h, w6_h, b6_h, wh_h, bh_h),
        (w1, b1, w2, b2, w3, b3, w4, b4, w5, b5, w6, b6, wh, bh),
    )
    for i, (src, dst) in enumerate(pairs):
        loads.append(pltpu.make_async_copy(src, dst, in_sem.at[1 + i]))
        loads[-1].start()

    rows = lax.broadcasted_iota(jnp.int32, (NY, NY), 0)
    mix[...] = jnp.where(rows % 4 * 128 + rows // 4 == lanes((NY, NY)), 1.0, 0.0).astype(BF16)
    load_d.wait()
    own = d_in[...].astype(F32).reshape(64, NY).astype(BF16)
    own = jnp.dot(own, mix[...], preferred_element_type=F32).reshape(8, 8, NY)
    dc[4:12] = own.astype(BF16)
    slo[...] = own[:, :4].astype(BF16)
    shi[...] = own[:, 4:].astype(BF16)
    pl.semaphore_wait(barrier, len(WAYS))

    edge_src = {-1: (0, 4), 0: (0, 8), 1: (4, 4)}
    edge_dst = {-1: (12, 4), 0: (4, 8), 1: (0, 4)}
    copies = []
    for k, (sz, sx) in enumerate(WAYS):
        z0, n = edge_src[sz]
        d0, _ = edge_dst[sz]
        if sx == 0:
            src, dst = dc.at[4 + z0 : 4 + z0 + n], dc.at[d0 : d0 + n]
        else:
            src = (slo if sx < 0 else shi).at[z0 : z0 + n]
            dst = (dr if sx < 0 else dl).at[d0 : d0 + n]
        copies.append(
            pltpu.make_async_remote_copy(
                src_ref=src, dst_ref=dst, send_sem=send1.at[k], recv_sem=recv1.at[k],
                device_id=neighbour((sz, sx)), device_id_type=MESH,
            )
        )
        copies[-1].start()

    for load in loads:
        load.wait()
    for k, (ref, count) in enumerate(((b1, 8), (b2, 8), (b3, 16), (b4, 16), (b5, 8), (b6, 8))):
        bias[k, :count, :] = jnp.broadcast_to(column(ref[...], count), (count, 128))

    taps = w1[...].astype(F32)
    shape = (14, 8, 256)
    lane = lanes(shape)
    slot = lane % 8
    rim = jnp.where(slot < 4, slot, slot + 8)
    xx = jnp.where(lane < 96, slot + 4, rim) - lax.broadcasted_iota(jnp.int32, shape, 0)
    place = jnp.where((xx >= 0) & (xx < 3), lane % 96 // 8 * 8 + xx, -1)
    acc = jnp.zeros(shape, F32)
    for dz in range(3):
        for dx in range(3):
            for dy in range(3):
                col = column(taps[dz * 3 + dx, dy : dy + 1, :], 8)
                acc = jnp.where(place == dz * 32 + dy * 8 + dx, jnp.broadcast_to(col[None], shape), acc)
    m1[...] = acc.reshape(112, 256).astype(BF16)

    tiles = spread_taps(w2[...], 256, 8)
    store_band(m2, tiles, 8, 4, 6)

    rows = lax.broadcasted_iota(jnp.int32, (8, 256), 0)
    table = (lanes((8, 256)) % 8 == rows).astype(F32).astype(BF16)
    w3v = w3[...]
    tiles = jnp.stack(
        [
            lax.dot_general(w3v[k], table, (((0,), (0,)), ((), ())), preferred_element_type=F32)
            for k in range(27)
        ]
    )
    store_band(m3, tiles, 8, 8, 10)
    store_band(m4, spread_taps(w4[...], 256, 16), 16, 3, 5)

    flat = w5[...].astype(F32).reshape(27 * 8, 24).astype(BF16)
    rows = lax.broadcasted_iota(jnp.int32, (24, 256), 0)
    lane = lanes((24, 256))
    table = (lane % 8 == rows).astype(F32).astype(BF16)
    tiles = jnp.dot(flat, table, preferred_element_type=F32).reshape(27, 8, 256)
    store_band(m5, tiles, 8, 4, 6)
    table = (lane % 16 + 8 == rows).astype(F32).astype(BF16)
    tiles = jnp.dot(flat, table, preferred_element_type=F32).reshape(27, 8, 256)
    shape = (10, 8, 256)
    coarse = lanes(shape) // 16
    out_x = lax.broadcasted_iota(jnp.int32, shape, 0)
    for odd in range(2):
        for dy in range(3):
            acc = jnp.zeros(shape, F32)
            for zc in range(2):
                for dx in range(3):
                    near = [dz for dz in range(3) if (dz + odd) // 2 == zc]
                    tile_v = sum(tiles[dz * 9 + dx * 3 + dy] for dz in near)
                    hit = coarse == zc * 6 + (out_x + dx) // 2
                    acc = acc + jnp.where(hit, jnp.broadcast_to(tile_v[None], shape), 0.0)
            at = odd * 240 + dy * 80
            m5c[at : at + 80, :] = acc.reshape(80, 256).astype(BF16)

    store_band(m6, spread_taps(w6[...], 256, 8), 8, 8, 10)

    rows = lax.broadcasted_iota(jnp.int32, (8, 128), 0)
    lane = lanes((8, 128))
    table = (lane % 8 == rows).astype(F32).astype(BF16)
    head = jnp.dot(wh[...], table, preferred_element_type=F32)
    mh[...] = jnp.where(lane // 8 == rows, jnp.broadcast_to(head, (8, 128)), 0.0).astype(BF16)

    lane = lanes((NY, NY))
    rows = lax.broadcasted_iota(jnp.int32, (NY, NY), 0)
    unmix[...] = jnp.where(lane % 4 * 128 + lane // 4 == rows, 1.0, 0.0).astype(BF16)

    wide_bias = jnp.concatenate([bias[0, :8, :]] * 4, axis=1)

    def turn(dst, z, rows8):
        part = [before(rows8), rows8, after(rows8), jnp.zeros_like(rows8)]
        dst[z] = jnp.concatenate(part, axis=0).astype(BF16)

    def turn_own(z):
        turn(own_y, z, dc[z].astype(F32))

    def turn_rim(z):
        turn(rim_y, z, jnp.concatenate([dl[z].astype(F32), dr[z].astype(F32)], axis=0))

    def first_own(z):
        total = jnp.dot(
            m1[32:80, :96], own_y[pl.ds(z, 3)].reshape(96, NY), preferred_element_type=F32
        )
        first[z, 32:80] = act(total.reshape(6, 8, NY) + wide_bias[None]).reshape(48, NY).astype(BF16)

    def first_rim(z):
        band = jnp.concatenate([m1[0:32, :192], m1[80:112, :192]], axis=0)
        window = jnp.concatenate(
            [own_y[pl.ds(z, 3)].reshape(96, NY), rim_y[pl.ds(z, 3)].reshape(96, NY)], axis=0
        )
        total = jnp.dot(band, window, preferred_element_type=F32).reshape(8, 8, NY)
        out = act(total + wide_bias[None]).reshape(64, NY).astype(BF16)
        first[z, 0:32] = out[:32]
        first[z, 80:112] = out[32:]

    def second(z, b):
        window = first[pl.ds(z, 3), 32 * b : 32 * b + 48].reshape(144, NY)
        out = fold(jnp.dot(m2[:, :144], window, preferred_element_type=F32), 32, bias[1, :8, :])
        skip[z, 32 * b : 32 * b + 32] = out
        return out.astype(F32)

    def pool(k, b):
        total = (second(2 * k, b) + second(2 * k + 1, b)).reshape(2, 2, 8, NY)
        total = total[:, 0] + total[:, 1]
        low = total[:, :, :128] + total[:, :, 128:256]
        high = total[:, :, 256:384] + total[:, :, 384:]
        mean = jnp.concatenate([low, high], axis=2) * 0.125
        pool_ex[2 + k, 2 + 2 * b : 4 + 2 * b] = mean.astype(BF16)

    pool_src = {-1: (4, 6), 0: (2, 8), 1: (4, 6)}
    pool_dst = {-1: (8, 10), 0: (2, 8), 1: (0, 2)}
    copies2 = []
    for k, (sz, sx) in enumerate(WAYS):
        (z0, z1), (x0, x1) = pool_src[sz], pool_src[sx]
        (y0, y1), (u0, u1) = pool_dst[sz], pool_dst[sx]
        copies2.append(
            pltpu.make_async_remote_copy(
                src_ref=pool_ex.at[z0:z1, x0:x1],
                dst_ref=pool_ex.at[y0:y1, u0:u1],
                send_sem=send2.at[k], recv_sem=recv2.at[k],
                device_id=neighbour((sz, sx)), device_id_type=MESH,
            )
        )

    for k, (sz, sx) in enumerate(WAYS):
        if sx == 0:
            copies[k].wait_recv()
    for z in range(16):
        turn_own(z)
    for z in range(14):
        first_own(z)
    for k in range(6):
        pool(k, 1)
    for k, (sz, sx) in enumerate(WAYS):
        if sx != 0:
            copies2[k].start()

    for k, (sz, sx) in enumerate(WAYS):
        if sx != 0:
            copies[k].wait_recv()
    for z in range(4, 12):
        turn_rim(z)
    for z in range(4, 10):
        first_rim(z)
    for k in (2, 3):
        pool(k, 0)
        pool(k, 2)
    for k, (sz, sx) in enumerate(WAYS):
        if sx == 0:
            copies2[k].start()

    for z in (0, 1, 2, 3, 12, 13, 14, 15):
        turn_rim(z)
    for z in (0, 1, 2, 3, 10, 11, 12, 13):
        first_rim(z)
    for k in (0, 1, 4, 5):
        pool(k, 0)
        pool(k, 2)

    def fifth_skip(z):
        for start, to, lo in ((0, 0, 0), (32, 32, 0), (48, 64, 16)):
            window = skip[pl.ds(z, 3), start : start + 48].reshape(144, NY)
            band = m5[:, :144]
            if lo:
                band = jnp.concatenate([band[16:32], band[48:64], band[80:96]], axis=0)
            n = 32 - lo
            fine[z, to : to + n] = gather(
                jnp.dot(band, window, preferred_element_type=F32), n, bias[4, :8, :]
            )

    for z in range(10):
        fifth_skip(z)

    for copy in copies:
        copy.wait_send()
    for copy in copies2:
        copy.wait()

    def repack(z):
        pooled[z] = pool_ex[z].astype(F32).reshape(80, NC).astype(BF16)

    def coarse_one(z):
        window = pooled[pl.ds(z, 3)].reshape(240, NC)
        one[z] = fold(
            jnp.dot(m3[:, :240], window, preferred_element_type=F32), 128, bias[2]
        )

    def coarse_two(z):
        for b in range(2):
            window = one[pl.ds(z, 3), 48 * b : 48 * b + 80].reshape(240, NC)
            two[z, 48 * b : 48 * b + 48] = fold(
                jnp.dot(m4[:, :240], window, preferred_element_type=F32), 48, bias[3]
            )

    def fifth(k):
        window = two[pl.ds(k, 2)].reshape(192, NC)
        parts = jnp.dot(m5c[:, :192], window, preferred_element_type=F32)
        for odd in range(2):
            a = [parts[240 * odd + 80 * dy : 240 * odd + 80 * dy + 80, :128] for dy in range(3)]
            b = [parts[240 * odd + 80 * dy : 240 * odd + 80 * dy + 80, 128:] for dy in range(3)]
            both = a[0] + b[2]
            blocks = [
                a[1] + a[2] + pltpu.roll(b[0], 1, 1),
                a[1] + both,
                b[1] + both,
                b[1] + b[0] + pltpu.roll(a[2], 127, 1),
            ]
            total = jnp.concatenate(blocks, axis=1) + fine[2 * k + odd]
            deco[2 * k + odd] = act(total).astype(BF16)

    def sixth(z):
        window = deco[pl.ds(z, 3)].reshape(240, NY)
        refined[z] = fold(
            jnp.dot(m6[:, :240], window, preferred_element_type=F32), 64, bias[5, :8, :]
        )

    loop(0, 10, UR, repack)
    loop(0, 8, U4, coarse_one)
    loop(0, 6, U5, coarse_two)
    loop(0, 5, U6, fifth)
    loop(0, 8, U7, sixth)
    head = jnp.concatenate(
        [jnp.dot(mh[:, :64], refined[z], preferred_element_type=F32) for z in range(8)], axis=0
    )
    head = head + jnp.broadcast_to(bh[...], (64, NY))
    parts = []
    for _ in range(3):
        parts.append(head.astype(BF16))
        head = head - parts[-1].astype(F32)
    plain = jnp.dot(jnp.concatenate(parts, axis=0), unmix[...], preferred_element_type=F32)
    out_ref[...] = (plain[:64] + plain[64:128] + plain[128:]).reshape(8, 8, NY)


def body(d, w1, b1, w2, b2, w3, b3, w4, b4, w5, b5, w6, b6, wh, bh):
    def taps(weight, order):
        turned = weight.transpose(order)
        return turned.reshape(27, turned.shape[3], turned.shape[4])

    plain, swapped = (2, 3, 4, 0, 1), (2, 3, 4, 1, 0)
    args = (
        d,
        w1.transpose(1, 2, 3, 4, 0).reshape(9, 3, 8), b1.reshape(1, 8),
        taps(w2, plain), b2.reshape(1, 8),
        taps(w3, swapped), b3.reshape(1, 16),
        taps(w4, plain), b4.reshape(1, 16),
        taps(w5, plain), b5.reshape(1, 8),
        taps(w6, plain), b6.reshape(1, 8),
        wh.reshape(1, 8), bh.reshape(1, 1),
    )
    V = pltpu.VMEM
    small = [V(a.shape, a.dtype) for a in args[1:]]
    return pl.pallas_call(
        kernel,
        out_shape=pltpu.VMEM((ZL, XL, NY), F32),
        in_specs=[pl.BlockSpec(memory_space=pl.ANY)] * len(args),
        out_specs=pl.BlockSpec(memory_space=pltpu.VMEM),
        scratch_shapes=small
        + [
            V((8, 8, NY), BF16), V((16, 8, NY), BF16), V((16, 4, NY), BF16), V((16, 4, NY), BF16),
            V((8, 4, NY), BF16), V((8, 4, NY), BF16),
            V((16, 32, NY), BF16), V((16, 32, NY), BF16),
            V((14, 112, NY), BF16), V((12, 96, NY), BF16),
            V((10, 10, 8, NC), BF16), V((10, 80, NC), BF16),
            V((8, 128, NC), BF16), V((6, 96, NC), BF16), V((10, 80, NY), F32), V((10, 80, NY), BF16), V((8, 64, NY), BF16),
            V((112, 256), BF16), V((96, 256), BF16),
            V((384, 256), BF16), V((144, 256), BF16), V((96, 256), BF16), V((480, 256), BF16),
            V((192, 256), BF16), V((8, 128), BF16),
            V((NY, NY), BF16), V((NY, NY), BF16), V((6, 16, 128), F32),
            pltpu.SemaphoreType.DMA((15,)),
            pltpu.SemaphoreType.DMA((8,)), pltpu.SemaphoreType.DMA((8,)),
            pltpu.SemaphoreType.DMA((8,)), pltpu.SemaphoreType.DMA((8,)),
        ],
        compiler_params=pltpu.CompilerParams(
            collective_id=0, has_side_effects=True, vmem_limit_bytes=67108864 - 196608
        ),
        name="unet_window",
    )(*args)


def solution(mesh):
    return jax.shard_map(
        body,
        mesh=mesh,
        in_specs=(P("gz", "tile", None),) + (P(),) * 14,
        out_specs=P("gz", "tile", None),
        check_vma=False,
    )
```

```python
import jax
import jax.numpy as jnp
from jax import lax
from jax.experimental import pallas as pl
from jax.experimental.pallas import tpu as pltpu
from jax.sharding import PartitionSpec as P

MESH = pl.DeviceIdType.MESH
F32 = jnp.float32
BF16 = jnp.bfloat16

ZL = 8
XL = 8
NY = 512
NC = NY // 2
WAYS = [(-1, -1), (-1, 1), (1, -1), (1, 1), (-1, 0), (1, 0), (0, -1), (0, 1)]

UR = 5
U4 = 8
U5 = 6
U6 = 5
U7 = 8


def lanes(shape):
    return lax.broadcasted_iota(jnp.int32, shape, len(shape) - 1)


def column(row, count):
    eye = lax.broadcasted_iota(jnp.int32, (count, count), 0) == lanes((count, count))
    return jnp.sum(jnp.where(eye, jnp.broadcast_to(row, (count, count)), 0.0), axis=1, keepdims=True)


def act(total):
    return jnp.maximum(total, 0.1 * total)


def spread_taps(weight, width, groups):
    taps, cout, cin = weight.shape
    rows = lax.broadcasted_iota(jnp.int32, (cin, width), 0)
    table = (lanes((cin, width)) % groups == rows).astype(F32).astype(BF16)
    flat = weight.astype(F32).reshape(taps * cout, cin).astype(BF16)
    return jnp.dot(flat, table, preferred_element_type=F32).reshape(taps, cout, width)


def store_band(dst, tiles, cin, outs, ins):
    cout, width = tiles.shape[1], tiles.shape[2]
    shape = (outs, cout, width)
    place = lanes(shape) // cin - lax.broadcasted_iota(jnp.int32, shape, 0)
    for dy in range(3):
        acc = jnp.zeros(shape, F32)
        for dz in range(3):
            for dx in range(3):
                tile = jnp.broadcast_to(tiles[dz * 9 + dx * 3 + dy][None], shape)
                acc = jnp.where(place == dz * ins + dx, tile, acc)
        rows = outs * cout
        dst[dy * rows : (dy + 1) * rows, :] = acc.reshape(rows, width).astype(BF16)


def loop(lo, hi, step, step_body):
    assert (hi - lo) % step == 0

    @pl.loop(0, (hi - lo) // step)
    def _(k):
        for u in range(step):
            step_body(lo + k * step + u)


def before(part):
    return jnp.concatenate([pltpu.roll(part[:, -128:], 1, 1), part[:, :-128]], axis=1)


def after(part):
    return jnp.concatenate([part[:, 128:], pltpu.roll(part[:, :128], 127, 1)], axis=1)


def gather(partial, rows, bias):
    width = partial.shape[1]
    total = partial[rows : 2 * rows] + before(partial[:rows]) + after(partial[2 * rows :])
    cout = bias.shape[0]
    bias = jnp.concatenate([bias] * (width // 128), axis=1)
    total = total.reshape(rows // cout, cout, width) + bias[None]
    return total.reshape(rows, width)


def fold(partial, rows, bias):
    return act(gather(partial, rows, bias)).astype(BF16)


def kernel(
    d_hbm, w1_h, b1_h, w2_h, b2_h, w3_h, b3_h, w4_h, b4_h, w5_h, b5_h, w6_h, b6_h, wh_h, bh_h,
    out_ref,
    w1, b1, w2, b2, w3, b3, w4, b4, w5, b5, w6, b6, wh, bh,
    d_in, dc, dl, dr, slo, shi, own_y, rim_y, first, skip, pool_ex, pooled, one, two, fine, deco, refined,
    m1, m2, m3, m4, m5, m5c, m6, mh, mix, unmix, bias,
    in_sem, send1, recv1, send2, recv2,
):
    gz, tile = lax.axis_size("gz"), lax.axis_size("tile")
    g, t = lax.axis_index("gz"), lax.axis_index("tile")

    def neighbour(way):
        return (lax.rem(g + way[0] + gz, gz), lax.rem(t + way[1] + tile, tile))

    barrier = pltpu.get_barrier_semaphore()
    for way in WAYS:
        pl.semaphore_signal(barrier, inc=1, device_id=neighbour(way), device_id_type=MESH)

    load_d = pltpu.make_async_copy(d_hbm, d_in, in_sem.at[0])
    load_d.start()
    loads = []
    pairs = zip(
        (w1_h, b1_h, w2_h, b2_h, w3_h, b3_h, w4_h, b4_h, w5_h, b5_h, w6_h, b6_h, wh_h, bh_h),
        (w1, b1, w2, b2, w3, b3, w4, b4, w5, b5, w6, b6, wh, bh),
    )
    for i, (src, dst) in enumerate(pairs):
        loads.append(pltpu.make_async_copy(src, dst, in_sem.at[1 + i]))
        loads[-1].start()

    rows = lax.broadcasted_iota(jnp.int32, (NY, NY), 0)
    mix[...] = jnp.where(rows % 4 * 128 + rows // 4 == lanes((NY, NY)), 1.0, 0.0).astype(BF16)
    load_d.wait()
    own = d_in[...].astype(F32).reshape(64, NY).astype(BF16)
    own = jnp.dot(own, mix[...], preferred_element_type=F32).reshape(8, 8, NY)
    dc[4:12] = own.astype(BF16)
    slo[...] = own[:, :4].astype(BF16)
    shi[...] = own[:, 4:].astype(BF16)
    pl.semaphore_wait(barrier, len(WAYS))

    edge_src = {-1: (0, 4), 0: (0, 8), 1: (4, 4)}
    edge_dst = {-1: (12, 4), 0: (4, 8), 1: (0, 4)}
    copies = []
    for k, (sz, sx) in enumerate(WAYS):
        z0, n = edge_src[sz]
        d0, _ = edge_dst[sz]
        if sx == 0:
            src, dst = dc.at[4 + z0 : 4 + z0 + n], dc.at[d0 : d0 + n]
        else:
            src = (slo if sx < 0 else shi).at[z0 : z0 + n]
            dst = (dr if sx < 0 else dl).at[d0 : d0 + n]
        copies.append(
            pltpu.make_async_remote_copy(
                src_ref=src, dst_ref=dst, send_sem=send1.at[k], recv_sem=recv1.at[k],
                device_id=neighbour((sz, sx)), device_id_type=MESH,
            )
        )
        copies[-1].start()

    for load in loads:
        load.wait()
    for k, (ref, count) in enumerate(((b1, 8), (b2, 8), (b3, 16), (b4, 16), (b5, 8), (b6, 8))):
        bias[k, :count, :] = jnp.broadcast_to(column(ref[...], count), (count, 128))

    taps = w1[...].astype(F32)
    shape = (14, 8, 256)
    lane = lanes(shape)
    slot = lane % 8
    rim = jnp.where(slot < 4, slot, slot + 8)
    xx = jnp.where(lane < 96, slot + 4, rim) - lax.broadcasted_iota(jnp.int32, shape, 0)
    place = jnp.where((xx >= 0) & (xx < 3), lane % 96 // 8 * 8 + xx, -1)
    acc = jnp.zeros(shape, F32)
    for dz in range(3):
        for dx in range(3):
            for dy in range(3):
                col = column(taps[dz * 3 + dx, dy : dy + 1, :], 8)
                acc = jnp.where(place == dz * 32 + dy * 8 + dx, jnp.broadcast_to(col[None], shape), acc)
    m1[...] = acc.reshape(112, 256).astype(BF16)

    tiles = spread_taps(w2[...], 256, 8)
    store_band(m2, tiles, 8, 4, 6)

    rows = lax.broadcasted_iota(jnp.int32, (8, 256), 0)
    table = (lanes((8, 256)) % 8 == rows).astype(F32).astype(BF16)
    w3v = w3[...]
    tiles = jnp.stack(
        [
            lax.dot_general(w3v[k], table, (((0,), (0,)), ((), ())), preferred_element_type=F32)
            for k in range(27)
        ]
    )
    store_band(m3, tiles, 8, 8, 10)
    store_band(m4, spread_taps(w4[...], 256, 16), 16, 3, 5)

    flat = w5[...].astype(F32).reshape(27 * 8, 24).astype(BF16)
    rows = lax.broadcasted_iota(jnp.int32, (24, 256), 0)
    lane = lanes((24, 256))
    table = (lane % 8 == rows).astype(F32).astype(BF16)
    tiles = jnp.dot(flat, table, preferred_element_type=F32).reshape(27, 8, 256)
    store_band(m5, tiles, 8, 4, 6)
    table = (lane % 16 + 8 == rows).astype(F32).astype(BF16)
    tiles = jnp.dot(flat, table, preferred_element_type=F32).reshape(27, 8, 256)
    shape = (10, 8, 256)
    coarse = lanes(shape) // 16
    out_x = lax.broadcasted_iota(jnp.int32, shape, 0)
    for odd in range(2):
        for dy in range(3):
            acc = jnp.zeros(shape, F32)
            for zc in range(2):
                for dx in range(3):
                    near = [dz for dz in range(3) if (dz + odd) // 2 == zc]
                    tile_v = sum(tiles[dz * 9 + dx * 3 + dy] for dz in near)
                    hit = coarse == zc * 6 + (out_x + dx) // 2
                    acc = acc + jnp.where(hit, jnp.broadcast_to(tile_v[None], shape), 0.0)
            at = odd * 240 + dy * 80
            m5c[at : at + 80, :] = acc.reshape(80, 256).astype(BF16)

    store_band(m6, spread_taps(w6[...], 256, 8), 8, 8, 10)

    rows = lax.broadcasted_iota(jnp.int32, (8, 128), 0)
    lane = lanes((8, 128))
    table = (lane % 8 == rows).astype(F32).astype(BF16)
    head = jnp.dot(wh[...], table, preferred_element_type=F32)
    mh[...] = jnp.where(lane // 8 == rows, jnp.broadcast_to(head, (8, 128)), 0.0).astype(BF16)

    lane = lanes((NY, NY))
    rows = lax.broadcasted_iota(jnp.int32, (NY, NY), 0)
    unmix[...] = jnp.where(lane % 4 * 128 + lane // 4 == rows, 1.0, 0.0).astype(BF16)

    wide_bias = jnp.concatenate([bias[0, :8, :]] * 4, axis=1)

    def turn(dst, z, rows8):
        part = [before(rows8), rows8, after(rows8), jnp.zeros_like(rows8)]
        dst[z] = jnp.concatenate(part, axis=0).astype(BF16)

    def turn_own(z):
        turn(own_y, z, dc[z].astype(F32))

    def turn_rim(z):
        turn(rim_y, z, jnp.concatenate([dl[z].astype(F32), dr[z].astype(F32)], axis=0))

    def first_own(z):
        total = jnp.dot(
            m1[32:80, :96], own_y[pl.ds(z, 3)].reshape(96, NY), preferred_element_type=F32
        )
        first[z, 32:80] = act(total.reshape(6, 8, NY) + wide_bias[None]).reshape(48, NY).astype(BF16)

    def first_rim(z):
        band = jnp.concatenate([m1[0:32, :192], m1[80:112, :192]], axis=0)
        window = jnp.concatenate(
            [own_y[pl.ds(z, 3)].reshape(96, NY), rim_y[pl.ds(z, 3)].reshape(96, NY)], axis=0
        )
        total = jnp.dot(band, window, preferred_element_type=F32).reshape(8, 8, NY)
        out = act(total + wide_bias[None]).reshape(64, NY).astype(BF16)
        first[z, 0:32] = out[:32]
        first[z, 80:112] = out[32:]

    def second(z, b):
        window = first[pl.ds(z, 3), 32 * b : 32 * b + 48].reshape(144, NY)
        out = fold(jnp.dot(m2[:, :144], window, preferred_element_type=F32), 32, bias[1, :8, :])
        skip[z, 32 * b : 32 * b + 32] = out
        return out.astype(F32)

    def pool(k, b):
        total = (second(2 * k, b) + second(2 * k + 1, b)).reshape(2, 2, 8, NY)
        total = total[:, 0] + total[:, 1]
        low = total[:, :, :128] + total[:, :, 128:256]
        high = total[:, :, 256:384] + total[:, :, 384:]
        mean = jnp.concatenate([low, high], axis=2) * 0.125
        pool_ex[2 + k, 2 + 2 * b : 4 + 2 * b] = mean.astype(BF16)

    pool_src = {-1: (4, 6), 0: (2, 8), 1: (4, 6)}
    pool_dst = {-1: (8, 10), 0: (2, 8), 1: (0, 2)}
    copies2 = []
    for k, (sz, sx) in enumerate(WAYS):
        (z0, z1), (x0, x1) = pool_src[sz], pool_src[sx]
        (y0, y1), (u0, u1) = pool_dst[sz], pool_dst[sx]
        copies2.append(
            pltpu.make_async_remote_copy(
                src_ref=pool_ex.at[z0:z1, x0:x1],
                dst_ref=pool_ex.at[y0:y1, u0:u1],
                send_sem=send2.at[k], recv_sem=recv2.at[k],
                device_id=neighbour((sz, sx)), device_id_type=MESH,
            )
        )

    for z in range(4, 12):
        turn_own(z)
    for z in range(4, 10):
        first_own(z)
    for k in (2, 3):
        pool(k, 1)

    def middle():
        for k, (sz, sx) in enumerate(WAYS):
            if sx == 0:
                copies[k].wait_recv()
        for z in (0, 1, 2, 3, 12, 13, 14, 15):
            turn_own(z)
        for z in (0, 1, 2, 3, 10, 11, 12, 13):
            first_own(z)
        for k in (0, 1, 4, 5):
            pool(k, 1)
        for k, (sz, sx) in enumerate(WAYS):
            if sx != 0:
                copies2[k].start()

    def layers():
        for k, (sz, sx) in enumerate(WAYS):
            if sz == 0:
                copies[k].wait_recv()
        for z in range(4, 12):
            turn_rim(z)
        for z in range(4, 10):
            first_rim(z)
        for k in (2, 3):
            pool(k, 0)
            pool(k, 2)
        for k, (sz, sx) in enumerate(WAYS):
            if sx == 0:
                copies2[k].start()

    row_start = lax.rem(t, 16) == 0

    @pl.when(row_start)
    def _():
        layers()
        middle()

    @pl.when(jnp.logical_not(row_start))
    def _():
        middle()
        layers()

    for k, (sz, sx) in enumerate(WAYS):
        if sz != 0 and sx != 0:
            copies[k].wait_recv()

    for z in (0, 1, 2, 3, 12, 13, 14, 15):
        turn_rim(z)
    for z in (0, 1, 2, 3, 10, 11, 12, 13):
        first_rim(z)
    for k in (0, 1, 4, 5):
        pool(k, 0)
        pool(k, 2)

    def fifth_skip(z):
        for start, to, lo in ((0, 0, 0), (32, 32, 0), (48, 64, 16)):
            window = skip[pl.ds(z, 3), start : start + 48].reshape(144, NY)
            band = m5[:, :144]
            if lo:
                band = jnp.concatenate([band[16:32], band[48:64], band[80:96]], axis=0)
            n = 32 - lo
            fine[z, to : to + n] = gather(
                jnp.dot(band, window, preferred_element_type=F32), n, bias[4, :8, :]
            )

    for z in range(10):
        fifth_skip(z)

    for copy in copies:
        copy.wait_send()
    for copy in copies2:
        copy.wait()

    def repack(z):
        pooled[z] = pool_ex[z].astype(F32).reshape(80, NC).astype(BF16)

    def coarse_one(z):
        window = pooled[pl.ds(z, 3)].reshape(240, NC)
        one[z] = fold(
            jnp.dot(m3[:, :240], window, preferred_element_type=F32), 128, bias[2]
        )

    def coarse_two(z):
        for b in range(2):
            window = one[pl.ds(z, 3), 48 * b : 48 * b + 80].reshape(240, NC)
            two[z, 48 * b : 48 * b + 48] = fold(
                jnp.dot(m4[:, :240], window, preferred_element_type=F32), 48, bias[3]
            )

    def fifth(k):
        window = two[pl.ds(k, 2)].reshape(192, NC)
        parts = jnp.dot(m5c[:, :192], window, preferred_element_type=F32)
        for odd in range(2):
            a = [parts[240 * odd + 80 * dy : 240 * odd + 80 * dy + 80, :128] for dy in range(3)]
            b = [parts[240 * odd + 80 * dy : 240 * odd + 80 * dy + 80, 128:] for dy in range(3)]
            both = a[0] + b[2]
            blocks = [
                a[1] + a[2] + pltpu.roll(b[0], 1, 1),
                a[1] + both,
                b[1] + both,
                b[1] + b[0] + pltpu.roll(a[2], 127, 1),
            ]
            total = jnp.concatenate(blocks, axis=1) + fine[2 * k + odd]
            deco[2 * k + odd] = act(total).astype(BF16)

    def sixth(z):
        window = deco[pl.ds(z, 3)].reshape(240, NY)
        refined[z] = fold(
            jnp.dot(m6[:, :240], window, preferred_element_type=F32), 64, bias[5, :8, :]
        )

    loop(0, 10, UR, repack)
    loop(0, 8, U4, coarse_one)
    loop(0, 6, U5, coarse_two)
    loop(0, 5, U6, fifth)
    loop(0, 8, U7, sixth)
    head = jnp.concatenate(
        [jnp.dot(mh[:, :64], refined[z], preferred_element_type=F32) for z in range(8)], axis=0
    )
    head = head + jnp.broadcast_to(bh[...], (64, NY))
    parts = []
    for _ in range(3):
        parts.append(head.astype(BF16))
        head = head - parts[-1].astype(F32)
    plain = jnp.dot(jnp.concatenate(parts, axis=0), unmix[...], preferred_element_type=F32)
    out_ref[...] = (plain[:64] + plain[64:128] + plain[128:]).reshape(8, 8, NY)


def body(d, w1, b1, w2, b2, w3, b3, w4, b4, w5, b5, w6, b6, wh, bh):
    def taps(weight, order):
        turned = weight.transpose(order)
        return turned.reshape(27, turned.shape[3], turned.shape[4])

    plain, swapped = (2, 3, 4, 0, 1), (2, 3, 4, 1, 0)
    args = (
        d,
        w1.transpose(1, 2, 3, 4, 0).reshape(9, 3, 8), b1.reshape(1, 8),
        taps(w2, plain), b2.reshape(1, 8),
        taps(w3, swapped), b3.reshape(1, 16),
        taps(w4, plain), b4.reshape(1, 16),
        taps(w5, plain), b5.reshape(1, 8),
        taps(w6, plain), b6.reshape(1, 8),
        wh.reshape(1, 8), bh.reshape(1, 1),
    )
    V = pltpu.VMEM
    small = [V(a.shape, a.dtype) for a in args[1:]]
    return pl.pallas_call(
        kernel,
        out_shape=pltpu.VMEM((ZL, XL, NY), F32),
        in_specs=[pl.BlockSpec(memory_space=pl.ANY)] * len(args),
        out_specs=pl.BlockSpec(memory_space=pltpu.VMEM),
        scratch_shapes=small
        + [
            V((8, 8, NY), BF16), V((16, 8, NY), BF16), V((16, 4, NY), BF16), V((16, 4, NY), BF16),
            V((8, 4, NY), BF16), V((8, 4, NY), BF16),
            V((16, 32, NY), BF16), V((16, 32, NY), BF16),
            V((14, 112, NY), BF16), V((12, 96, NY), BF16),
            V((10, 10, 8, NC), BF16), V((10, 80, NC), BF16),
            V((8, 128, NC), BF16), V((6, 96, NC), BF16), V((10, 80, NY), F32), V((10, 80, NY), BF16), V((8, 64, NY), BF16),
            V((112, 256), BF16), V((96, 256), BF16),
            V((384, 256), BF16), V((144, 256), BF16), V((96, 256), BF16), V((480, 256), BF16),
            V((192, 256), BF16), V((8, 128), BF16),
            V((NY, NY), BF16), V((NY, NY), BF16), V((6, 16, 128), F32),
            pltpu.SemaphoreType.DMA((15,)),
            pltpu.SemaphoreType.DMA((8,)), pltpu.SemaphoreType.DMA((8,)),
            pltpu.SemaphoreType.DMA((8,)), pltpu.SemaphoreType.DMA((8,)),
        ],
        compiler_params=pltpu.CompilerParams(
            collective_id=0, has_side_effects=True, vmem_limit_bytes=67108864 - 196608
        ),
        name="unet_window",
    )(*args)


def solution(mesh):
    return jax.shard_map(
        body,
        mesh=mesh,
        in_specs=(P("gz", "tile", None),) + (P(),) * 14,
        out_specs=P("gz", "tile", None),
        check_vma=False,
    )
```

```python
import jax
import jax.numpy as jnp
from jax import lax
from jax.experimental import pallas as pl
from jax.experimental.pallas import tpu as pltpu
from jax.sharding import PartitionSpec as P

MESH = pl.DeviceIdType.MESH
F32 = jnp.float32
BF16 = jnp.bfloat16

ZL = 8
XL = 8
NY = 512
NC = NY // 2
WAYS = [(-1, -1), (-1, 1), (1, -1), (1, 1), (-1, 0), (1, 0), (0, -1), (0, 1)]

UR = 5
U4 = 8
U5 = 6
U6 = 5
U7 = 8


def lanes(shape):
    return lax.broadcasted_iota(jnp.int32, shape, len(shape) - 1)


def column(row, count):
    eye = lax.broadcasted_iota(jnp.int32, (count, count), 0) == lanes((count, count))
    return jnp.sum(jnp.where(eye, jnp.broadcast_to(row, (count, count)), 0.0), axis=1, keepdims=True)


def act(total):
    return jnp.maximum(total, 0.1 * total)


def spread_taps(weight, width, groups):
    taps, cout, cin = weight.shape
    rows = lax.broadcasted_iota(jnp.int32, (cin, width), 0)
    table = (lanes((cin, width)) % groups == rows).astype(F32).astype(BF16)
    flat = weight.astype(F32).reshape(taps * cout, cin).astype(BF16)
    return jnp.dot(flat, table, preferred_element_type=F32).reshape(taps, cout, width)


def store_band(dst, tiles, cin, outs, ins):
    cout, width = tiles.shape[1], tiles.shape[2]
    shape = (outs, cout, width)
    place = lanes(shape) // cin - lax.broadcasted_iota(jnp.int32, shape, 0)
    for dy in range(3):
        acc = jnp.zeros(shape, F32)
        for dz in range(3):
            for dx in range(3):
                tile = jnp.broadcast_to(tiles[dz * 9 + dx * 3 + dy][None], shape)
                acc = jnp.where(place == dz * ins + dx, tile, acc)
        rows = outs * cout
        dst[dy * rows : (dy + 1) * rows, :] = acc.reshape(rows, width).astype(BF16)


def loop(lo, hi, step, step_body):
    assert (hi - lo) % step == 0

    @pl.loop(0, (hi - lo) // step)
    def _(k):
        for u in range(step):
            step_body(lo + k * step + u)


def before(part):
    return jnp.concatenate([pltpu.roll(part[:, -128:], 1, 1), part[:, :-128]], axis=1)


def after(part):
    return jnp.concatenate([part[:, 128:], pltpu.roll(part[:, :128], 127, 1)], axis=1)


def gather(partial, rows, bias):
    width = partial.shape[1]
    total = partial[rows : 2 * rows] + before(partial[:rows]) + after(partial[2 * rows :])
    cout = bias.shape[0]
    bias = jnp.concatenate([bias] * (width // 128), axis=1)
    total = total.reshape(rows // cout, cout, width) + bias[None]
    return total.reshape(rows, width)


def fold(partial, rows, bias):
    return act(gather(partial, rows, bias)).astype(BF16)


def kernel(
    d_hbm, w1_h, b1_h, w2_h, b2_h, w3_h, b3_h, w4_h, b4_h, w5_h, b5_h, w6_h, b6_h, wh_h, bh_h,
    out_ref,
    w1, b1, w2, b2, w3, b3, w4, b4, w5, b5, w6, b6, wh, bh,
    d_in, dc, dl, dr, slo, shi, own_y, rim_y, first, skip, pool_ex, pooled, one, two, fine, deco, refined,
    m1, m2, m3, m4, m5, m5c, m6, mh, mix, unmix, bias,
    in_sem, send1, recv1, send2, recv2,
):
    gz, tile = lax.axis_size("gz"), lax.axis_size("tile")
    g, t = lax.axis_index("gz"), lax.axis_index("tile")

    def neighbour(way):
        return (lax.rem(g + way[0] + gz, gz), lax.rem(t + way[1] + tile, tile))

    barrier = pltpu.get_barrier_semaphore()
    for way in WAYS:
        pl.semaphore_signal(barrier, inc=1, device_id=neighbour(way), device_id_type=MESH)

    load_d = pltpu.make_async_copy(d_hbm, d_in, in_sem.at[0])
    load_d.start()
    loads = []
    pairs = zip(
        (w1_h, b1_h, w2_h, b2_h, w3_h, b3_h, w4_h, b4_h, w5_h, b5_h, w6_h, b6_h, wh_h, bh_h),
        (w1, b1, w2, b2, w3, b3, w4, b4, w5, b5, w6, b6, wh, bh),
    )
    for i, (src, dst) in enumerate(pairs):
        loads.append(pltpu.make_async_copy(src, dst, in_sem.at[1 + i]))
        loads[-1].start()

    rows = lax.broadcasted_iota(jnp.int32, (NY, NY), 0)
    mix[...] = jnp.where(rows % 4 * 128 + rows // 4 == lanes((NY, NY)), 1.0, 0.0).astype(BF16)
    load_d.wait()
    own = d_in[...].astype(F32).reshape(64, NY).astype(BF16)
    own = jnp.dot(own, mix[...], preferred_element_type=F32).reshape(8, 8, NY)
    dc[4:12] = own.astype(BF16)
    slo[...] = own[:, :4].astype(BF16)
    shi[...] = own[:, 4:].astype(BF16)
    pl.semaphore_wait(barrier, len(WAYS))

    edge_src = {-1: (0, 4), 0: (0, 8), 1: (4, 4)}
    edge_dst = {-1: (12, 4), 0: (4, 8), 1: (0, 4)}
    copies = []
    for k, (sz, sx) in enumerate(WAYS):
        z0, n = edge_src[sz]
        d0, _ = edge_dst[sz]
        if sx == 0:
            src, dst = dc.at[4 + z0 : 4 + z0 + n], dc.at[d0 : d0 + n]
        else:
            src = (slo if sx < 0 else shi).at[z0 : z0 + n]
            dst = (dr if sx < 0 else dl).at[d0 : d0 + n]
        copies.append(
            pltpu.make_async_remote_copy(
                src_ref=src, dst_ref=dst, send_sem=send1.at[k], recv_sem=recv1.at[k],
                device_id=neighbour((sz, sx)), device_id_type=MESH,
            )
        )
        copies[-1].start()

    for load in loads:
        load.wait()
    for k, (ref, count) in enumerate(((b1, 8), (b2, 8), (b3, 16), (b4, 16), (b5, 8), (b6, 8))):
        bias[k, :count, :] = jnp.broadcast_to(column(ref[...], count), (count, 128))

    taps = w1[...].astype(F32)
    shape = (14, 8, 256)
    lane = lanes(shape)
    slot = lane % 8
    rim = jnp.where(slot < 4, slot, slot + 8)
    xx = jnp.where(lane < 96, slot + 4, rim) - lax.broadcasted_iota(jnp.int32, shape, 0)
    place = jnp.where((xx >= 0) & (xx < 3), lane % 96 // 8 * 8 + xx, -1)
    acc = jnp.zeros(shape, F32)
    for dz in range(3):
        for dx in range(3):
            for dy in range(3):
                col = column(taps[dz * 3 + dx, dy : dy + 1, :], 8)
                acc = jnp.where(place == dz * 32 + dy * 8 + dx, jnp.broadcast_to(col[None], shape), acc)
    m1[...] = acc.reshape(112, 256).astype(BF16)

    tiles = spread_taps(w2[...], 256, 8)
    store_band(m2, tiles, 8, 4, 6)

    rows = lax.broadcasted_iota(jnp.int32, (8, 256), 0)
    table = (lanes((8, 256)) % 8 == rows).astype(F32).astype(BF16)
    w3v = w3[...]
    tiles = jnp.stack(
        [
            lax.dot_general(w3v[k], table, (((0,), (0,)), ((), ())), preferred_element_type=F32)
            for k in range(27)
        ]
    )
    store_band(m3, tiles, 8, 8, 10)
    store_band(m4, spread_taps(w4[...], 256, 16), 16, 3, 5)

    flat = w5[...].astype(F32).reshape(27 * 8, 24).astype(BF16)
    rows = lax.broadcasted_iota(jnp.int32, (24, 256), 0)
    lane = lanes((24, 256))
    table = (lane % 8 == rows).astype(F32).astype(BF16)
    tiles = jnp.dot(flat, table, preferred_element_type=F32).reshape(27, 8, 256)
    store_band(m5, tiles, 8, 4, 6)
    table = (lane % 16 + 8 == rows).astype(F32).astype(BF16)
    tiles = jnp.dot(flat, table, preferred_element_type=F32).reshape(27, 8, 256)
    shape = (10, 8, 256)
    coarse = lanes(shape) // 16
    out_x = lax.broadcasted_iota(jnp.int32, shape, 0)
    for odd in range(2):
        for dy in range(3):
            acc = jnp.zeros(shape, F32)
            for zc in range(2):
                for dx in range(3):
                    near = [dz for dz in range(3) if (dz + odd) // 2 == zc]
                    tile_v = sum(tiles[dz * 9 + dx * 3 + dy] for dz in near)
                    hit = coarse == zc * 6 + (out_x + dx) // 2
                    acc = acc + jnp.where(hit, jnp.broadcast_to(tile_v[None], shape), 0.0)
            at = odd * 240 + dy * 80
            m5c[at : at + 80, :] = acc.reshape(80, 256).astype(BF16)

    store_band(m6, spread_taps(w6[...], 256, 8), 8, 8, 10)

    rows = lax.broadcasted_iota(jnp.int32, (8, 128), 0)
    lane = lanes((8, 128))
    table = (lane % 8 == rows).astype(F32).astype(BF16)
    head = jnp.dot(wh[...], table, preferred_element_type=F32)
    mh[...] = jnp.where(lane // 8 == rows, jnp.broadcast_to(head, (8, 128)), 0.0).astype(BF16)

    lane = lanes((NY, NY))
    rows = lax.broadcasted_iota(jnp.int32, (NY, NY), 0)
    unmix[...] = jnp.where(lane % 4 * 128 + lane // 4 == rows, 1.0, 0.0).astype(BF16)

    wide_bias = jnp.concatenate([bias[0, :8, :]] * 4, axis=1)

    def turn(dst, z, rows8):
        part = [before(rows8), rows8, after(rows8), jnp.zeros_like(rows8)]
        dst[z] = jnp.concatenate(part, axis=0).astype(BF16)

    def turn_own(z):
        turn(own_y, z, dc[z].astype(F32))

    def turn_rim(z):
        turn(rim_y, z, jnp.concatenate([dl[z].astype(F32), dr[z].astype(F32)], axis=0))

    def first_own(z):
        total = jnp.dot(
            m1[32:80, :96], own_y[pl.ds(z, 3)].reshape(96, NY), preferred_element_type=F32
        )
        first[z, 32:80] = act(total.reshape(6, 8, NY) + wide_bias[None]).reshape(48, NY).astype(BF16)

    def first_rim(z):
        band = jnp.concatenate([m1[0:32, :192], m1[80:112, :192]], axis=0)
        window = jnp.concatenate(
            [own_y[pl.ds(z, 3)].reshape(96, NY), rim_y[pl.ds(z, 3)].reshape(96, NY)], axis=0
        )
        total = jnp.dot(band, window, preferred_element_type=F32).reshape(8, 8, NY)
        out = act(total + wide_bias[None]).reshape(64, NY).astype(BF16)
        first[z, 0:32] = out[:32]
        first[z, 80:112] = out[32:]

    def second(z, b):
        window = first[pl.ds(z, 3), 32 * b : 32 * b + 48].reshape(144, NY)
        out = fold(jnp.dot(m2[:, :144], window, preferred_element_type=F32), 32, bias[1, :8, :])
        skip[z, 32 * b : 32 * b + 32] = out
        return out.astype(F32)

    def pool(k, b):
        total = (second(2 * k, b) + second(2 * k + 1, b)).reshape(2, 2, 8, NY)
        total = total[:, 0] + total[:, 1]
        low = total[:, :, :128] + total[:, :, 128:256]
        high = total[:, :, 256:384] + total[:, :, 384:]
        mean = jnp.concatenate([low, high], axis=2) * 0.125
        pool_ex[2 + k, 2 + 2 * b : 4 + 2 * b] = mean.astype(BF16)

    pool_src = {-1: (4, 6), 1: (4, 6)}
    pool_dst = {-1: (8, 10), 1: (0, 2)}
    pieces = [(way, pool_src[way[0]], pool_src[way[1]]) for way in WAYS[:4]]
    pieces += [((sz, 0), (4, 6), (4, 6)) for sz in (-1, 1)]
    pieces += [((0, sx), (2, 8), (4, 6)) for sx in (-1, 1)]
    pieces += [((sz, 0), (4, 6), (x, x + 2)) for sz in (-1, 1) for x in (2, 6)]
    copies2 = []
    for k, ((sz, sx), (z0, z1), (x0, x1)) in enumerate(pieces):
        y0, y1 = pool_dst.get(sz, (z0, z1))
        u0, u1 = pool_dst.get(sx, (x0, x1))
        copies2.append(
            pltpu.make_async_remote_copy(
                src_ref=pool_ex.at[z0:z1, x0:x1],
                dst_ref=pool_ex.at[y0:y1, u0:u1],
                send_sem=send2.at[k], recv_sem=recv2.at[k],
                device_id=neighbour((sz, sx)), device_id_type=MESH,
            )
        )

    for z in range(4, 12):
        turn_own(z)
    for z in range(4, 10):
        first_own(z)
    for k in (2, 3):
        pool(k, 1)
    for copy in copies2[:6]:
        copy.start()

    def middle():
        for k, (sz, sx) in enumerate(WAYS):
            if sx == 0:
                copies[k].wait_recv()
        for z in (0, 1, 2, 3, 12, 13, 14, 15):
            turn_own(z)
        for z in (0, 1, 2, 3, 10, 11, 12, 13):
            first_own(z)
        for k in (0, 1, 4, 5):
            pool(k, 1)
        for copy in copies2[6:8]:
            copy.start()

    def layers():
        for k, (sz, sx) in enumerate(WAYS):
            if sz == 0:
                copies[k].wait_recv()
        for z in range(4, 12):
            turn_rim(z)
        for z in range(4, 10):
            first_rim(z)
        for k in (2, 3):
            pool(k, 0)
            pool(k, 2)
        for copy in copies2[8:]:
            copy.start()

    row_start = lax.rem(t, 16) == 0

    @pl.when(row_start)
    def _():
        layers()
        middle()

    @pl.when(jnp.logical_not(row_start))
    def _():
        middle()
        layers()

    for k, (sz, sx) in enumerate(WAYS):
        if sz != 0 and sx != 0:
            copies[k].wait_recv()

    for z in (0, 1, 2, 3, 12, 13, 14, 15):
        turn_rim(z)
    for z in (0, 1, 2, 3, 10, 11, 12, 13):
        first_rim(z)
    for k in (0, 1, 4, 5):
        pool(k, 0)
        pool(k, 2)

    def fifth_skip(z):
        for start, to, lo in ((0, 0, 0), (32, 32, 0), (48, 64, 16)):
            window = skip[pl.ds(z, 3), start : start + 48].reshape(144, NY)
            band = m5[:, :144]
            if lo:
                band = jnp.concatenate([band[16:32], band[48:64], band[80:96]], axis=0)
            n = 32 - lo
            fine[z, to : to + n] = gather(
                jnp.dot(band, window, preferred_element_type=F32), n, bias[4, :8, :]
            )

    for z in range(10):
        fifth_skip(z)

    for copy in copies:
        copy.wait_send()
    for copy in copies2:
        copy.wait()

    def repack(z):
        pooled[z] = pool_ex[z].astype(F32).reshape(80, NC).astype(BF16)

    def coarse_one(z):
        window = pooled[pl.ds(z, 3)].reshape(240, NC)
        one[z] = fold(
            jnp.dot(m3[:, :240], window, preferred_element_type=F32), 128, bias[2]
        )

    def coarse_two(z):
        for b in range(2):
            window = one[pl.ds(z, 3), 48 * b : 48 * b + 80].reshape(240, NC)
            two[z, 48 * b : 48 * b + 48] = fold(
                jnp.dot(m4[:, :240], window, preferred_element_type=F32), 48, bias[3]
            )

    def fifth(k):
        window = two[pl.ds(k, 2)].reshape(192, NC)
        parts = jnp.dot(m5c[:, :192], window, preferred_element_type=F32)
        for odd in range(2):
            a = [parts[240 * odd + 80 * dy : 240 * odd + 80 * dy + 80, :128] for dy in range(3)]
            b = [parts[240 * odd + 80 * dy : 240 * odd + 80 * dy + 80, 128:] for dy in range(3)]
            both = a[0] + b[2]
            blocks = [
                a[1] + a[2] + pltpu.roll(b[0], 1, 1),
                a[1] + both,
                b[1] + both,
                b[1] + b[0] + pltpu.roll(a[2], 127, 1),
            ]
            total = jnp.concatenate(blocks, axis=1) + fine[2 * k + odd]
            deco[2 * k + odd] = act(total).astype(BF16)

    def sixth(z):
        window = deco[pl.ds(z, 3)].reshape(240, NY)
        refined[z] = fold(
            jnp.dot(m6[:, :240], window, preferred_element_type=F32), 64, bias[5, :8, :]
        )

    loop(0, 10, UR, repack)
    loop(0, 8, U4, coarse_one)
    loop(0, 6, U5, coarse_two)
    loop(0, 5, U6, fifth)
    loop(0, 8, U7, sixth)
    head = jnp.concatenate(
        [jnp.dot(mh[:, :64], refined[z], preferred_element_type=F32) for z in range(8)], axis=0
    )
    head = head + jnp.broadcast_to(bh[...], (64, NY))
    parts = []
    for _ in range(3):
        parts.append(head.astype(BF16))
        head = head - parts[-1].astype(F32)
    plain = jnp.dot(jnp.concatenate(parts, axis=0), unmix[...], preferred_element_type=F32)
    out_ref[...] = (plain[:64] + plain[64:128] + plain[128:]).reshape(8, 8, NY)


def body(d, w1, b1, w2, b2, w3, b3, w4, b4, w5, b5, w6, b6, wh, bh):
    def taps(weight, order):
        turned = weight.transpose(order)
        return turned.reshape(27, turned.shape[3], turned.shape[4])

    plain, swapped = (2, 3, 4, 0, 1), (2, 3, 4, 1, 0)
    args = (
        d,
        w1.transpose(1, 2, 3, 4, 0).reshape(9, 3, 8), b1.reshape(1, 8),
        taps(w2, plain), b2.reshape(1, 8),
        taps(w3, swapped), b3.reshape(1, 16),
        taps(w4, plain), b4.reshape(1, 16),
        taps(w5, plain), b5.reshape(1, 8),
        taps(w6, plain), b6.reshape(1, 8),
        wh.reshape(1, 8), bh.reshape(1, 1),
    )
    V = pltpu.VMEM
    small = [V(a.shape, a.dtype) for a in args[1:]]
    return pl.pallas_call(
        kernel,
        out_shape=pltpu.VMEM((ZL, XL, NY), F32),
        in_specs=[pl.BlockSpec(memory_space=pl.ANY)] * len(args),
        out_specs=pl.BlockSpec(memory_space=pltpu.VMEM),
        scratch_shapes=small
        + [
            V((8, 8, NY), BF16), V((16, 8, NY), BF16), V((16, 4, NY), BF16), V((16, 4, NY), BF16),
            V((8, 4, NY), BF16), V((8, 4, NY), BF16),
            V((16, 32, NY), BF16), V((16, 32, NY), BF16),
            V((14, 112, NY), BF16), V((12, 96, NY), BF16),
            V((10, 10, 8, NC), BF16), V((10, 80, NC), BF16),
            V((8, 128, NC), BF16), V((6, 96, NC), BF16), V((10, 80, NY), F32), V((10, 80, NY), BF16), V((8, 64, NY), BF16),
            V((112, 256), BF16), V((96, 256), BF16),
            V((384, 256), BF16), V((144, 256), BF16), V((96, 256), BF16), V((480, 256), BF16),
            V((192, 256), BF16), V((8, 128), BF16),
            V((NY, NY), BF16), V((NY, NY), BF16), V((6, 16, 128), F32),
            pltpu.SemaphoreType.DMA((15,)),
            pltpu.SemaphoreType.DMA((8,)), pltpu.SemaphoreType.DMA((8,)),
            pltpu.SemaphoreType.DMA((12,)), pltpu.SemaphoreType.DMA((12,)),
        ],
        compiler_params=pltpu.CompilerParams(
            collective_id=0, has_side_effects=True, vmem_limit_bytes=67108864 - 196608
        ),
        name="unet_window",
    )(*args)


def solution(mesh):
    return jax.shard_map(
        body,
        mesh=mesh,
        in_specs=(P("gz", "tile", None),) + (P(),) * 14,
        out_specs=P("gz", "tile", None),
        check_vma=False,
    )
```

```python
import jax
import jax.numpy as jnp
from jax import lax
from jax.experimental import pallas as pl
from jax.experimental.pallas import tpu as pltpu
from jax.sharding import PartitionSpec as P

MESH = pl.DeviceIdType.MESH
F32 = jnp.float32
BF16 = jnp.bfloat16

ZL = 8
XL = 8
NY = 512
NC = NY // 2
WAYS = [(-1, -1), (-1, 1), (1, -1), (1, 1), (-1, 0), (1, 0), (0, -1), (0, 1)]

UR = 5
U4 = 8
U5 = 6
U6 = 5
U7 = 8


def lanes(shape):
    return lax.broadcasted_iota(jnp.int32, shape, len(shape) - 1)


def column(row, count):
    eye = lax.broadcasted_iota(jnp.int32, (count, count), 0) == lanes((count, count))
    return jnp.sum(jnp.where(eye, jnp.broadcast_to(row, (count, count)), 0.0), axis=1, keepdims=True)


def act(total):
    return jnp.maximum(total, 0.1 * total)


def spread_taps(weight, width, groups):
    taps, cout, cin = weight.shape
    rows = lax.broadcasted_iota(jnp.int32, (cin, width), 0)
    table = (lanes((cin, width)) % groups == rows).astype(F32).astype(BF16)
    flat = weight.astype(F32).reshape(taps * cout, cin).astype(BF16)
    return jnp.dot(flat, table, preferred_element_type=F32).reshape(taps, cout, width)


def store_band(dst, tiles, cin, outs, ins):
    cout, width = tiles.shape[1], tiles.shape[2]
    shape = (outs, cout, width)
    place = lanes(shape) // cin - lax.broadcasted_iota(jnp.int32, shape, 0)
    for dy in range(3):
        acc = jnp.zeros(shape, F32)
        for dz in range(3):
            for dx in range(3):
                tile = jnp.broadcast_to(tiles[dz * 9 + dx * 3 + dy][None], shape)
                acc = jnp.where(place == dz * ins + dx, tile, acc)
        rows = outs * cout
        dst[dy * rows : (dy + 1) * rows, :] = acc.reshape(rows, width).astype(BF16)


def loop(lo, hi, step, step_body):
    assert (hi - lo) % step == 0

    @pl.loop(0, (hi - lo) // step)
    def _(k):
        for u in range(step):
            step_body(lo + k * step + u)


def before(part):
    return jnp.concatenate([pltpu.roll(part[:, -128:], 1, 1), part[:, :-128]], axis=1)


def after(part):
    return jnp.concatenate([part[:, 128:], pltpu.roll(part[:, :128], 127, 1)], axis=1)


def gather(partial, rows, bias):
    width = partial.shape[1]
    total = partial[rows : 2 * rows] + before(partial[:rows]) + after(partial[2 * rows :])
    cout = bias.shape[0]
    bias = jnp.concatenate([bias] * (width // 128), axis=1)
    total = total.reshape(rows // cout, cout, width) + bias[None]
    return total.reshape(rows, width)


def fold(partial, rows, bias):
    return act(gather(partial, rows, bias)).astype(BF16)


def kernel(
    d_hbm, w1_h, b1_h, w2_h, b2_h, w3_h, b3_h, w4_h, b4_h, w5_h, b5_h, w6_h, b6_h, wh_h, bh_h,
    out_ref,
    w1, b1, w2, b2, w3, b3, w4, b4, w5, b5, w6, b6, wh, bh,
    d_in, dc, dl, dr, slo, shi, own_y, rim_y, first, skip, pool_ex, pooled, one, two, fine, deco, refined,
    m1, m2, m3, m4, m5, m5c, m6, mh, mix, unmix, bias,
    in_sem, send1, recv1, send2, recv2,
):
    gz, tile = lax.axis_size("gz"), lax.axis_size("tile")
    g, t = lax.axis_index("gz"), lax.axis_index("tile")

    def neighbour(way):
        return (lax.rem(g + way[0] + gz, gz), lax.rem(t + way[1] + tile, tile))

    barrier = pltpu.get_barrier_semaphore()
    for way in WAYS:
        pl.semaphore_signal(barrier, inc=1, device_id=neighbour(way), device_id_type=MESH)

    load_d = pltpu.make_async_copy(d_hbm, d_in, in_sem.at[0])
    load_d.start()
    loads = []
    pairs = zip(
        (w1_h, b1_h, w2_h, b2_h, w3_h, b3_h, w4_h, b4_h, w5_h, b5_h, w6_h, b6_h, wh_h, bh_h),
        (w1, b1, w2, b2, w3, b3, w4, b4, w5, b5, w6, b6, wh, bh),
    )
    for i, (src, dst) in enumerate(pairs):
        loads.append(pltpu.make_async_copy(src, dst, in_sem.at[1 + i]))
        loads[-1].start()

    rows = lax.broadcasted_iota(jnp.int32, (NY, NY), 0)
    mix[...] = jnp.where(rows % 4 * 128 + rows // 4 == lanes((NY, NY)), 1.0, 0.0).astype(BF16)
    load_d.wait()
    own = d_in[...].astype(F32).reshape(64, NY).astype(BF16)
    own = jnp.dot(own, mix[...], preferred_element_type=F32).reshape(8, 8, NY)
    dc[4:12] = own.astype(BF16)
    slo[...] = own[:, :4].astype(BF16)
    shi[...] = own[:, 4:].astype(BF16)
    pl.semaphore_wait(barrier, len(WAYS))

    edge_src = {-1: (0, 4), 0: (0, 8), 1: (4, 4)}
    edge_dst = {-1: (12, 4), 0: (4, 8), 1: (0, 4)}
    copies = []
    for k, (sz, sx) in enumerate(WAYS):
        z0, n = edge_src[sz]
        d0, _ = edge_dst[sz]
        if sx == 0:
            src, dst = dc.at[4 + z0 : 4 + z0 + n], dc.at[d0 : d0 + n]
        else:
            src = (slo if sx < 0 else shi).at[z0 : z0 + n]
            dst = (dr if sx < 0 else dl).at[d0 : d0 + n]
        copies.append(
            pltpu.make_async_remote_copy(
                src_ref=src, dst_ref=dst, send_sem=send1.at[k], recv_sem=recv1.at[k],
                device_id=neighbour((sz, sx)), device_id_type=MESH,
            )
        )
        copies[-1].start()

    for load in loads:
        load.wait()
    for k, (ref, count) in enumerate(((b1, 8), (b2, 8), (b3, 16), (b4, 16), (b5, 8), (b6, 8))):
        bias[k, :count, :] = jnp.broadcast_to(column(ref[...], count), (count, 128))

    taps = w1[...].astype(F32)
    shape = (14, 8, 256)
    lane = lanes(shape)
    slot = lane % 8
    rim = jnp.where(slot < 4, slot, slot + 8)
    xx = jnp.where(lane < 96, slot + 4, rim) - lax.broadcasted_iota(jnp.int32, shape, 0)
    place = jnp.where((xx >= 0) & (xx < 3), lane % 96 // 8 * 8 + xx, -1)
    acc = jnp.zeros(shape, F32)
    for dz in range(3):
        for dx in range(3):
            for dy in range(3):
                col = column(taps[dz * 3 + dx, dy : dy + 1, :], 8)
                acc = jnp.where(place == dz * 32 + dy * 8 + dx, jnp.broadcast_to(col[None], shape), acc)
    m1[...] = acc.reshape(112, 256).astype(BF16)

    tiles = spread_taps(w2[...], 256, 8)
    store_band(m2, tiles, 8, 4, 6)

    rows = lax.broadcasted_iota(jnp.int32, (8, 256), 0)
    table = (lanes((8, 256)) % 8 == rows).astype(F32).astype(BF16)
    w3v = w3[...]
    tiles = jnp.stack(
        [
            lax.dot_general(w3v[k], table, (((0,), (0,)), ((), ())), preferred_element_type=F32)
            for k in range(27)
        ]
    )
    store_band(m3, tiles, 8, 8, 10)
    store_band(m4, spread_taps(w4[...], 256, 16), 16, 3, 5)

    flat = w5[...].astype(F32).reshape(27 * 8, 24).astype(BF16)
    rows = lax.broadcasted_iota(jnp.int32, (24, 256), 0)
    lane = lanes((24, 256))
    table = (lane % 8 == rows).astype(F32).astype(BF16)
    tiles = jnp.dot(flat, table, preferred_element_type=F32).reshape(27, 8, 256)
    store_band(m5, tiles, 8, 4, 6)
    table = (lane % 16 + 8 == rows).astype(F32).astype(BF16)
    tiles = jnp.dot(flat, table, preferred_element_type=F32).reshape(27, 8, 256)
    shape = (10, 8, 256)
    coarse = lanes(shape) // 16
    out_x = lax.broadcasted_iota(jnp.int32, shape, 0)
    for odd in range(2):
        for dy in range(3):
            acc = jnp.zeros(shape, F32)
            for zc in range(2):
                for dx in range(3):
                    near = [dz for dz in range(3) if (dz + odd) // 2 == zc]
                    tile_v = sum(tiles[dz * 9 + dx * 3 + dy] for dz in near)
                    hit = coarse == zc * 6 + (out_x + dx) // 2
                    acc = acc + jnp.where(hit, jnp.broadcast_to(tile_v[None], shape), 0.0)
            at = odd * 240 + dy * 80
            m5c[at : at + 80, :] = acc.reshape(80, 256).astype(BF16)

    store_band(m6, spread_taps(w6[...], 256, 8), 8, 8, 10)

    rows = lax.broadcasted_iota(jnp.int32, (8, 128), 0)
    lane = lanes((8, 128))
    table = (lane % 8 == rows).astype(F32).astype(BF16)
    head = jnp.dot(wh[...], table, preferred_element_type=F32)
    mh[...] = jnp.where(lane // 8 == rows, jnp.broadcast_to(head, (8, 128)), 0.0).astype(BF16)

    lane = lanes((NY, NY))
    rows = lax.broadcasted_iota(jnp.int32, (NY, NY), 0)
    unmix[...] = jnp.where(lane % 4 * 128 + lane // 4 == rows, 1.0, 0.0).astype(BF16)

    wide_bias = jnp.concatenate([bias[0, :8, :]] * 4, axis=1)

    def turn(dst, z, rows8):
        part = [before(rows8), rows8, after(rows8), jnp.zeros_like(rows8)]
        dst[z] = jnp.concatenate(part, axis=0).astype(BF16)

    def turn_own(z):
        turn(own_y, z, dc[z].astype(F32))

    def turn_rim(z):
        turn(rim_y, z, jnp.concatenate([dl[z].astype(F32), dr[z].astype(F32)], axis=0))

    def first_own(z):
        total = jnp.dot(
            m1[32:80, :96], own_y[pl.ds(z, 3)].reshape(96, NY), preferred_element_type=F32
        )
        first[z, 32:80] = act(total.reshape(6, 8, NY) + wide_bias[None]).reshape(48, NY).astype(BF16)

    def first_rim(z):
        band = jnp.concatenate([m1[0:32, :192], m1[80:112, :192]], axis=0)
        window = jnp.concatenate(
            [own_y[pl.ds(z, 3)].reshape(96, NY), rim_y[pl.ds(z, 3)].reshape(96, NY)], axis=0
        )
        total = jnp.dot(band, window, preferred_element_type=F32).reshape(8, 8, NY)
        out = act(total + wide_bias[None]).reshape(64, NY).astype(BF16)
        first[z, 0:32] = out[:32]
        first[z, 80:112] = out[32:]

    def second(z, b):
        window = first[pl.ds(z, 3), 32 * b : 32 * b + 48].reshape(144, NY)
        out = fold(jnp.dot(m2[:, :144], window, preferred_element_type=F32), 32, bias[1, :8, :])
        skip[z, 32 * b : 32 * b + 32] = out
        return out.astype(F32)

    def pool(k, b):
        total = (second(2 * k, b) + second(2 * k + 1, b)).reshape(2, 2, 8, NY)
        total = total[:, 0] + total[:, 1]
        low = total[:, :, :128] + total[:, :, 128:256]
        high = total[:, :, 256:384] + total[:, :, 384:]
        mean = jnp.concatenate([low, high], axis=2) * 0.125
        pool_ex[2 + k, 2 + 2 * b : 4 + 2 * b] = mean.astype(BF16)

    pool_src = {-1: (4, 6), 1: (4, 6)}
    pool_dst = {-1: (8, 10), 1: (0, 2)}
    pieces = [(way, pool_src[way[0]], pool_src[way[1]]) for way in WAYS[:4]]
    pieces += [((sz, 0), (4, 6), (4, 6)) for sz in (-1, 1)]
    pieces += [((0, sx), (2, 8), (4, 6)) for sx in (-1, 1)]
    pieces += [((sz, 0), (4, 6), (x, x + 2)) for sz in (-1, 1) for x in (2, 6)]
    copies2 = []
    for k, ((sz, sx), (z0, z1), (x0, x1)) in enumerate(pieces):
        y0, y1 = pool_dst.get(sz, (z0, z1))
        u0, u1 = pool_dst.get(sx, (x0, x1))
        copies2.append(
            pltpu.make_async_remote_copy(
                src_ref=pool_ex.at[z0:z1, x0:x1],
                dst_ref=pool_ex.at[y0:y1, u0:u1],
                send_sem=send2.at[k], recv_sem=recv2.at[k],
                device_id=neighbour((sz, sx)), device_id_type=MESH,
            )
        )

    for z in range(4, 12):
        turn_own(z)
    for z in range(4, 10):
        first_own(z)
    for k in (2, 3):
        pool(k, 1)
    for copy in copies2[:6]:
        copy.start()

    def middle():
        for k, (sz, sx) in enumerate(WAYS):
            if sx == 0:
                copies[k].wait_recv()
        for z in (0, 1, 2, 3, 12, 13, 14, 15):
            turn_own(z)
        for z in (0, 1, 2, 3, 10, 11, 12, 13):
            first_own(z)
        for k in (0, 1, 4, 5):
            pool(k, 1)
        for copy in copies2[6:8]:
            copy.start()

    def layers():
        for k, (sz, sx) in enumerate(WAYS):
            if sz == 0:
                copies[k].wait_recv()
        for z in range(4, 12):
            turn_rim(z)
        for z in range(4, 10):
            first_rim(z)
        for k in (2, 3):
            pool(k, 0)
            pool(k, 2)
        for copy in copies2[8:]:
            copy.start()

    row_start = lax.rem(t, 16) == 0

    @pl.when(row_start)
    def _():
        layers()
        middle()

    @pl.when(jnp.logical_not(row_start))
    def _():
        middle()
        layers()

    for k, (sz, sx) in enumerate(WAYS):
        if sz != 0 and sx != 0:
            copies[k].wait_recv()

    for z in (0, 1, 2, 3, 12, 13, 14, 15):
        turn_rim(z)
    for z in (0, 1, 2, 3, 10, 11, 12, 13):
        first_rim(z)
    for k in (0, 1, 4, 5):
        pool(k, 0)
        pool(k, 2)

    def fifth_skip(z):
        for start, to, lo in ((0, 0, 0), (32, 32, 0), (48, 64, 16)):
            window = skip[pl.ds(z, 3), start : start + 48].reshape(144, NY)
            band = m5[:, :144]
            if lo:
                band = jnp.concatenate([band[16:32], band[48:64], band[80:96]], axis=0)
            n = 32 - lo
            fine[z, to : to + n] = gather(
                jnp.dot(band, window, preferred_element_type=F32), n, bias[4, :8, :]
            )

    for z in range(10):
        fifth_skip(z)

    for copy in copies:
        copy.wait_send()
    for copy in copies2:
        copy.wait()

    def repack(z):
        pooled[z] = pool_ex[z].astype(F32).reshape(80, NC).astype(BF16)

    def coarse_one(z):
        window = pooled[pl.ds(z, 3)].reshape(240, NC)
        one[z] = fold(
            jnp.dot(m3[:, :240], window, preferred_element_type=F32), 128, bias[2]
        )

    def coarse_two(z):
        for b in range(2):
            window = one[pl.ds(z, 3), 48 * b : 48 * b + 80].reshape(240, NC)
            two[z, 48 * b : 48 * b + 48] = fold(
                jnp.dot(m4[:, :240], window, preferred_element_type=F32), 48, bias[3]
            )

    def fifth(k):
        window = two[pl.ds(k, 2)].reshape(192, NC)
        parts = jnp.dot(m5c[:, :192], window, preferred_element_type=F32)
        for odd in range(2):
            a = [parts[240 * odd + 80 * dy : 240 * odd + 80 * dy + 80, :128] for dy in range(3)]
            b = [parts[240 * odd + 80 * dy : 240 * odd + 80 * dy + 80, 128:] for dy in range(3)]
            both = a[0] + b[2]
            blocks = [
                a[1] + a[2] + pltpu.roll(b[0], 1, 1),
                a[1] + both,
                b[1] + both,
                b[1] + b[0] + pltpu.roll(a[2], 127, 1),
            ]
            total = jnp.concatenate(blocks, axis=1) + fine[2 * k + odd]
            deco[2 * k + odd] = act(total).astype(BF16)

    def sixth(z):
        window = deco[pl.ds(z, 3)].reshape(240, NY)
        refined[z] = fold(
            jnp.dot(m6[:, :240], window, preferred_element_type=F32), 64, bias[5, :8, :]
        )

    loop(0, 10, UR, repack)
    loop(0, 8, U4, coarse_one)
    loop(0, 6, U5, coarse_two)
    loop(0, 5, U6, fifth)
    loop(0, 8, U7, sixth)
    head = jnp.concatenate(
        [jnp.dot(mh[:, :64], refined[z], preferred_element_type=F32) for z in range(8)], axis=0
    )
    head = head + jnp.broadcast_to(bh[...], (64, NY))
    parts = []
    for _ in range(2):
        parts.append(head.astype(BF16))
        head = head - parts[-1].astype(F32)
    plain = jnp.dot(jnp.concatenate(parts, axis=0), unmix[...], preferred_element_type=F32)
    out_ref[...] = (plain[:64] + plain[64:]).reshape(8, 8, NY)


def body(d, w1, b1, w2, b2, w3, b3, w4, b4, w5, b5, w6, b6, wh, bh):
    def taps(weight, order):
        turned = weight.transpose(order)
        return turned.reshape(27, turned.shape[3], turned.shape[4])

    plain, swapped = (2, 3, 4, 0, 1), (2, 3, 4, 1, 0)
    args = (
        d,
        w1.transpose(1, 2, 3, 4, 0).reshape(9, 3, 8), b1.reshape(1, 8),
        taps(w2, plain), b2.reshape(1, 8),
        taps(w3, swapped), b3.reshape(1, 16),
        taps(w4, plain), b4.reshape(1, 16),
        taps(w5, plain), b5.reshape(1, 8),
        taps(w6, plain), b6.reshape(1, 8),
        wh.reshape(1, 8), bh.reshape(1, 1),
    )
    V = pltpu.VMEM
    small = [V(a.shape, a.dtype) for a in args[1:]]
    return pl.pallas_call(
        kernel,
        out_shape=pltpu.VMEM((ZL, XL, NY), F32),
        in_specs=[pl.BlockSpec(memory_space=pl.ANY)] * len(args),
        out_specs=pl.BlockSpec(memory_space=pltpu.VMEM),
        scratch_shapes=small
        + [
            V((8, 8, NY), BF16), V((16, 8, NY), BF16), V((16, 4, NY), BF16), V((16, 4, NY), BF16),
            V((8, 4, NY), BF16), V((8, 4, NY), BF16),
            V((16, 32, NY), BF16), V((16, 32, NY), BF16),
            V((14, 112, NY), BF16), V((12, 96, NY), BF16),
            V((10, 10, 8, NC), BF16), V((10, 80, NC), BF16),
            V((8, 128, NC), BF16), V((6, 96, NC), BF16), V((10, 80, NY), F32), V((10, 80, NY), BF16), V((8, 64, NY), BF16),
            V((112, 256), BF16), V((96, 256), BF16),
            V((384, 256), BF16), V((144, 256), BF16), V((96, 256), BF16), V((480, 256), BF16),
            V((192, 256), BF16), V((8, 128), BF16),
            V((NY, NY), BF16), V((NY, NY), BF16), V((6, 16, 128), F32),
            pltpu.SemaphoreType.DMA((15,)),
            pltpu.SemaphoreType.DMA((8,)), pltpu.SemaphoreType.DMA((8,)),
            pltpu.SemaphoreType.DMA((12,)), pltpu.SemaphoreType.DMA((12,)),
        ],
        compiler_params=pltpu.CompilerParams(
            collective_id=0, has_side_effects=True, vmem_limit_bytes=67108864 - 196608
        ),
        name="unet_window",
    )(*args)


def solution(mesh):
    return jax.shard_map(
        body,
        mesh=mesh,
        in_specs=(P("gz", "tile", None),) + (P(),) * 14,
        out_specs=P("gz", "tile", None),
        check_vma=False,
    )
```
